32 devices in a mesh: section: 4 (over y, x), seq: 8 (over z, core).
Axes of the slice: x: 2, y: 2, z: 4, core: 2. Of those that a mesh axis runs over, the one named last changes fastest.
Arguments:
- tokens: bfloat16 [4096, 2048], P('seq', 'section'), may hold values from -6 to 6
- norm_gain: float32 [2048], replicated, may hold values from 0.25 to 1.75
- w_query: bfloat16 [2048, 2048], P('seq', 'section'), may hold values from -0.3125 to 0.3125
- w_key: bfloat16 [2048, 512], P('seq', 'section'), may hold values from -0.125 to 0.125
- w_value: bfloat16 [2048, 512], P('seq', 'section'), may hold values from -0.125 to 0.125
- w_out: bfloat16 [2048, 2048], P('seq', 'section'), may hold values from -0.25 to 0.25
- router_gate: float32 [4096], P('seq'), may hold values from 0.25 to 1
- chosen_blocks: int32 [8, 1], replicated, may hold values from 0 to 3, as said below
- block_counts: int32 [8], replicated, may hold values from 0 to 1, as said below
Outputs:
- mixed: bfloat16 [4096, 2048], P('seq', 'section')
The draws below stay inside these ranges and needn't reach their ends.
Inputs may be any that keep to these rules, and one draw needn't show every extreme that they name: `chosen_blocks`: in each segment's row the entries name distinct blocks of 128 rows of that segment, in increasing order; only the first block_counts entries are used. `block_counts`: some segment has one chosen block and some segment has none.
All inputs are finite; a program needn't handle non-finite values.
Results may differ from the reference program's by a relative error of at most 0.0034.
Values may be sent and summed in bfloat16 or wider, within the bound.
A program may use at most 64 MiB of HBM per device.

```python
import jax
import jax.numpy as jnp
from jax import lax

D = 2048
HEADS = 16
KV_HEADS = 4
HEAD_DIM = 128
BLOCK = 128
TOK_DEV = 512
CAP = 128
TOKENS = 4096
N_SEQ = 8


def route_plan(key):
    base = jax.random.fold_in(key, 4321)
    first_key, second_key, third_key, fourth_key = jax.random.split(base, 4)
    segment_total = TOKENS // TOK_DEV
    block_total = TOK_DEV // BLOCK
    most_blocks = TOK_DEV // (4 * BLOCK)
    counts = jax.random.randint(first_key, (segment_total,), 0, most_blocks + 1)
    full_at = jax.random.randint(second_key, (), 0, segment_total)
    empty_at = (full_at + 1 + jax.random.randint(third_key, (), 0, segment_total - 1)) % segment_total
    segment_index = jnp.arange(segment_total)
    counts = jnp.where(segment_index == full_at, most_blocks, jnp.where(segment_index == empty_at, 0, counts))
    ranking = jax.random.randint(fourth_key, (segment_total, block_total), 0, 1 << 20) * block_total + jnp.arange(block_total)[None, :]
    ordering = jnp.argsort(ranking, axis=1)[:, :most_blocks]
    blocks = jnp.sort(ordering, axis=1)
    return (blocks.astype(jnp.int32), counts.astype(jnp.int32))


def draw_chosen_blocks(key, part):
    return route_plan(key)[0]


def draw_block_counts(key, part):
    return route_plan(key)[1]


def steps_of(own_key, dims, cuts, smallest, top_value):
    level = 1.0
    for position, parts in cuts:
        steps = jax.random.uniform(jax.random.fold_in(jax.random.fold_in(own_key, 6), position), (parts,), jnp.float32, smallest / len(cuts), top_value / len(cuts))
        level = level * jnp.repeat(jnp.exp(steps), dims[position] // parts).reshape((-1,) + (1,) * (len(dims) - 1 - position))
    return level


def noise(own_key, shape, scale, bound, pieces=(), held_as=jnp.bfloat16):
    result = jax.random.normal(own_key, shape, jnp.float32) * scale
    if len(pieces) > 0:
        result = steps_of(own_key, shape, pieces, -0.22, 0.18) * result
    return jnp.clip(result, min=-bound, max=bound).astype(held_as)


def setup_inputs(seed: int = 0) -> dict:
    splits = jax.random.split(jax.random.key(seed), 10)
    tokens = noise(splits[0], (TOKENS, D), 1.0, 6.0, ((0, 8), (1, 4)))
    norm_gain = jnp.clip(1.0 + 0.15 * jax.random.normal(splits[1], (D,), jnp.float32), 0.25, 1.75)
    w_query = noise(splits[2], (D, HEADS * HEAD_DIM), (D // 6) ** -0.5, 0.3125, ((0, 8), (1, 4)))
    w_key = noise(splits[3], (D, KV_HEADS * HEAD_DIM), D ** -0.5, 0.125, ((0, 8), (1, 4)))
    w_value = noise(splits[4], (D, KV_HEADS * HEAD_DIM), D ** -0.5, 0.125, ((0, 8), (1, 4)))
    w_out = noise(splits[5], (HEADS * HEAD_DIM, D), (HEADS * HEAD_DIM // 4) ** -0.5, 0.25, ((0, 8), (1, 4)))
    router_gate = jnp.clip(0.25 + 0.75 * jax.random.uniform(splits[6], (TOKENS,), jnp.float32) ** steps_of(splits[6], (TOKENS,), ((0, 8),), -0.2, 0.2), 0.25, 1.0)
    chosen_blocks = draw_chosen_blocks(jax.random.fold_in(splits[9], 71), 0)
    block_counts = draw_block_counts(jax.random.fold_in(splits[9], 71), 0)
    return dict(tokens=tokens, norm_gain=norm_gain, w_query=w_query, w_key=w_key, w_value=w_value, w_out=w_out, router_gate=router_gate, chosen_blocks=chosen_blocks, block_counts=block_counts)


EPSILON = 1e-05

def reference(tokens, norm_gain, w_query, w_key, w_value, w_out, router_gate, chosen_blocks, block_counts):
    slot_index = jnp.arange(CAP, dtype=jnp.int32)
    slot_block = slot_index // BLOCK
    local_rows = jnp.take(chosen_blocks, slot_block, axis=1).astype(jnp.int32) * BLOCK + (slot_index % BLOCK)[None, :]
    segment_first = (jnp.arange(N_SEQ, dtype=jnp.int32) * TOK_DEV)[:, None]
    places = (segment_first + local_rows).reshape(-1)
    live_slots = (slot_block[None, :] < block_counts[:, None]).reshape(-1)
    key_places = jnp.where(live_slots, places, TOKENS)
    picked = jnp.take(tokens, places, axis=0)
    features = picked.astype(jnp.float32)
    normed = (features * lax.rsqrt(lax.optimization_barrier(jnp.mean(features * features, axis=-1, keepdims=True)) + EPSILON) * norm_gain).astype(jnp.bfloat16)
    queries = jnp.dot(normed, w_query, preferred_element_type=jnp.float32).astype(jnp.bfloat16)
    key_rows = jnp.dot(normed, w_key, preferred_element_type=jnp.float32).astype(jnp.bfloat16)
    value_rows = jnp.dot(normed, w_value, preferred_element_type=jnp.float32).astype(jnp.bfloat16)
    repeat_count = HEADS // KV_HEADS
    slots_total = N_SEQ * CAP
    keys_wide = lax.optimization_barrier(key_rows).astype(jnp.float32).reshape(slots_total, KV_HEADS, HEAD_DIM)
    values_wide = lax.optimization_barrier(value_rows).astype(jnp.float32).reshape(slots_total, KV_HEADS, HEAD_DIM)
    queries_wide = lax.optimization_barrier(queries).astype(jnp.float32).reshape(N_SEQ, CAP, KV_HEADS, repeat_count, HEAD_DIM)
    score_scale = HEAD_DIM ** (-0.5)

    def one_segment(packed):
        segment_queries, segment_places, segment_live = packed
        scores = jnp.einsum('qgrd,kgd->grqk', segment_queries, keys_wide) * score_scale
        allowed = key_places[None, :] <= segment_places[:, None]
        weights = jnp.where(allowed[None, None], jnp.exp(scores), 0.0)
        denominators = lax.optimization_barrier(jnp.sum(weights, axis=-1))
        rounded = lax.optimization_barrier(weights.astype(jnp.bfloat16)).astype(jnp.float32)
        summed = jnp.einsum('grqk,kgd->qgrd', rounded, values_wide)
        safe = jnp.where(segment_live[None, None, :], denominators, 1.0)
        return (summed / jnp.transpose(safe, (2, 0, 1))[..., None]).astype(jnp.bfloat16)
    attended = lax.map(one_segment, (queries_wide, places.reshape(N_SEQ, CAP), live_slots.reshape(N_SEQ, CAP)))
    attended = attended.reshape(slots_total, HEADS * HEAD_DIM)
    update = jnp.dot(attended, w_out, preferred_element_type=jnp.float32)
    gate_rows = jnp.take(router_gate, places)
    new_rows = (features + gate_rows[:, None] * update).astype(jnp.bfloat16)
    targets = jnp.where(live_slots, places, TOKENS)
    return tokens.at[targets].set(new_rows, mode='drop')
```

```python
import functools
import math

import jax
import jax.numpy as jnp
from jax import lax
from jax.experimental import pallas as pl
from jax.experimental.pallas import tpu as pltpu
from jax.sharding import PartitionSpec as P

HEADS = 16
KV_HEADS = 4
HEAD_DIM = 128
BLOCK = 128
EPSILON = 1e-05
MESH = pl.DeviceIdType.MESH

KV, QUERY, OUT_A, OUT_B = range(4)
CHUNKS = (KV, QUERY, OUT_A, OUT_B)


def repeat(low, high, body):
    if high - low <= 4:
        for step in range(low, high):
            body(step)
    else:

        def wrapped(step, carry):
            body(step)
            return carry

        lax.fori_loop(low, high, wrapped, 0)


def kernel(
    seq_count,
    section_count,
    tile_spots,
    tokens_ref,
    gain_ref,
    gate_ref,
    chosen_ref,
    count_ref,
    wq_in,
    wk_in,
    wv_in,
    wo_in,
    out_ref,
    rows_all,
    gate_rows,
    normed_ref,
    wkv,
    wq,
    wo,
    panel,
    queries_ref,
    numer_ref,
    denom_ref,
    heads_all,
    results,
    returned,
    key_slots,
    weight_send,
    weight_recv,
    rows_send,
    rows_pair,
    rows_recv,
    gate_send,
    gate_recv,
    panel_line,
    panel_pair,
    panel_recv,
    heads_send,
    heads_pair,
    heads_recv,
    back_send,
    back_recv,
):
    me = lax.axis_index("seq")
    section = lax.axis_index("section")
    line = seq_count // 2
    spot = me // 2
    core = lax.rem(me, 2)
    pair = spot * 2 + 1 - core
    slots = chosen_ref.shape[0] // seq_count
    capacity, width = out_ref.shape
    chip_rows = 2 * capacity
    kv_cols = wk_in.shape[1]
    ratio = HEADS // KV_HEADS
    half_q = wq_in.shape[1] // 2
    heads_half = half_q // HEAD_DIM
    half_o = wo_in.shape[1] // 2
    part_o = half_o // 2
    depth = section_count * width
    first, last = 1, line - 2
    active = (spot >= first) & (spot <= last)
    has_guest = (spot == first) | (spot == last)
    near = jnp.where(spot * 2 < line, 1, -1)
    guest_spot = spot - near
    host_spot = spot + near
    spots = (spot, guest_spot)

    def for_who(body):
        body(0)
        pl.when(has_guest)(lambda: body(1))

    def host_of(place):
        if isinstance(place, int):
            return min(max(place, first), last)
        return jnp.clip(place, first, last)

    def rows_of(block, size):
        return pl.ds(pl.multiple_of(block * size, size), size)

    def remote(src, dst, send, receive, **device):
        return pltpu.make_async_remote_copy(
            src_ref=src,
            dst_ref=dst,
            send_sem=send,
            recv_sem=receive,
            device_id=device,
            device_id_type=MESH,
        )

    def others(body):
        for offset in range(1, section_count):
            body(offset, lax.rem(section + offset, section_count))

    def weight_from(chunk, half):
        if chunk == KV:
            return (wk_in, wv_in)[half]
        if chunk == QUERY:
            return wq_in.at[:, pl.ds(half * half_q, half_q)]
        return wo_in.at[:, pl.ds(half * half_o + (chunk - OUT_A) * part_o, part_o)]

    def weight_to(chunk, block):
        if chunk == KV:
            return wkv.at[rows_of(block, wk_in.shape[0]), :]
        if chunk == QUERY:
            return wq.at[rows_of(block, wq_in.shape[0]), :]
        return wo.at[chunk - OUT_A, rows_of(block, wo_in.shape[0]), :]

    def weight_copy(chunk, half, target):
        return remote(
            weight_from(chunk, half),
            weight_to(chunk, me),
            weight_send.at[chunk, target],
            weight_recv.at[chunk, me],
            seq=target,
        )

    def send_weight(chunk):
        def body(host):
            for half in range(2):
                target = host * 2 + half

                @pl.when(target != me)
                def _():
                    weight_copy(chunk, half, target).start()

                @pl.when(target == me)
                def _():
                    pltpu.make_async_copy(
                        weight_from(chunk, half), weight_to(chunk, me), weight_recv.at[chunk, me]
                    ).start()

        repeat(first, last + 1, body)

    def finish_weight(chunk):
        def body(host):
            for half in range(2):
                target = host * 2 + half

                @pl.when(target != me)
                def _():
                    weight_copy(chunk, half, target).wait_send()

        repeat(first, last + 1, body)

    def await_weight(chunk):
        def body(block):
            pltpu.make_async_copy(
                weight_to(chunk, block), weight_to(chunk, block), weight_recv.at[chunk, block]
            ).wait()

        for block in range(0, seq_count) if seq_count <= 8 else ():
            body(block)
        if seq_count > 8:
            repeat(0, seq_count, body)

    def rows_copy(part, place, send, **device):
        return remote(
            rows_all.at[part, place],
            rows_all.at[part, place],
            send,
            rows_recv.at[place, part],
            **device,
        )

    def rows_spread(who, offset, peer):
        return rows_copy(section, who * 2 + core, rows_send.at[who, offset], section=peer)

    def rows_to_pair(who, part):
        return rows_copy(part, who * 2 + core, rows_pair.at[who, part], seq=pair)

    def await_rows(part, place):
        rows_copy(part, place, rows_send.at[0, 0], seq=pair).wait_recv()

    def guest_copies():
        copies = [
            remote(
                rows_all.at[section, core],
                rows_all.at[section, 2 + core],
                rows_send.at[0, 0],
                rows_recv.at[2 + core, section],
                seq=host_spot * 2 + core,
            )
        ]
        for half in range(2):
            copies.append(
                remote(
                    gate_rows.at[core],
                    gate_rows.at[2 + core],
                    gate_send.at[half],
                    gate_recv.at[2 + core],
                    seq=host_spot * 2 + half,
                )
            )
        return copies

    def gate_copy(place):
        return remote(
            gate_rows.at[place], gate_rows.at[place], gate_send.at[0], gate_recv.at[place], seq=pair
        )

    def panel_copy(kind, place, send, target):
        piece = panel.at[kind, rows_of(place, chip_rows), :]
        return remote(piece, piece, send, panel_recv.at[kind, place], seq=target)

    def panel_to_pair(place):
        return panel_copy(core, place, panel_pair.at[place], pair)

    def panel_onward(who, host):
        return panel_copy(core, spots[who], panel_line.at[who, host], host * 2 + core)

    def later_hosts(body):
        def guarded(host):
            pl.when(host > spot)(lambda: body(host))

        repeat(first, last + 1, guarded)

    def await_panel(kind, place):
        panel_copy(kind, place, panel_pair.at[place], pair).wait_recv()

    def earlier_spots(body):
        def guarded(place):
            pl.when(host_of(place) < spot)(lambda: body(place))

        repeat(0, line, guarded)

    def heads_copy(part, half, who, send, **device):
        piece = heads_all.at[part, half, who]
        return remote(piece, piece, send, heads_recv.at[who, half, part], **device)

    def heads_spread(who, offset, peer):
        return heads_copy(section, core, who, heads_send.at[who, offset], section=peer)

    def heads_to_pair(who, part):
        return heads_copy(part, core, who, heads_pair.at[who, part], seq=pair)

    def await_heads(who, half, part):
        heads_copy(part, half, who, heads_send.at[0, 0], seq=pair).wait_recv()

    def give_back(place, part, target):
        return remote(
            results.at[place, part],
            returned.at[core, part],
            back_send.at[place, part],
            back_recv.at[core, part],
            seq=target,
        )

    def await_back(half, part):
        remote(
            returned.at[half, part],
            returned.at[half, part],
            back_send.at[0, part],
            back_recv.at[half, part],
            seq=pair,
        ).wait_recv()

    for slot in range(slots):
        number = chosen_ref[me * slots + slot]
        rows = tokens_ref[:BLOCK, :]
        gates = gate_ref[:1, :]
        for block in range(1, gate_ref.shape[0]):
            rows = jnp.where(
                jnp.full(rows.shape, number, jnp.int32) == block,
                tokens_ref[block * BLOCK : (block + 1) * BLOCK, :],
                rows,
            )
            gates = jnp.where(
                jnp.full(gates.shape, number, jnp.int32) == block,
                gate_ref[block : block + 1, :],
                gates,
            )
        rows_all[section, core, pl.ds(slot * BLOCK, BLOCK), :] = rows
        gate_rows[core, pl.ds(slot, 1), :] = gates

    barrier = pltpu.get_barrier_semaphore()

    def greet(other):
        @pl.when((other != me) & (active | (other >= first * 2) & (other < (last + 1) * 2)))
        def _():
            pl.semaphore_signal(barrier, inc=1, device_id={"seq": other}, device_id_type=MESH)

    for other in range(seq_count) if seq_count <= 8 else ():
        greet(other)
    if seq_count > 8:
        repeat(0, seq_count, greet)

    @pl.when(active)
    def _():
        others(
            lambda offset, peer: pl.semaphore_signal(
                barrier, inc=1, device_id={"section": peer}, device_id_type=MESH
            )
        )

    hosts = (last - first + 1) * 2
    pl.semaphore_wait(barrier, jnp.where(active, seq_count - 1 + section_count - 1, hosts))

    @pl.when(jnp.logical_not(active))
    def _():
        for copy in guest_copies():
            copy.start()
        for chunk in CHUNKS:
            send_weight(chunk)

    def gate_column(place):
        wide = gate_rows[place]
        square = lax.broadcasted_iota(jnp.int32, (BLOCK, BLOCK), 0) == lax.broadcasted_iota(
            jnp.int32, (BLOCK, BLOCK), 1
        )
        return jnp.concatenate(
            [
                jnp.sum(jnp.where(square, wide[slot : slot + 1, :], 0.0), axis=1, keepdims=True)
                for slot in range(slots)
            ],
            axis=0,
        )

    def normalise(place):
        square_sum = jnp.zeros((capacity, 1), jnp.float32)
        for part in range(section_count):
            features = rows_all[part, place].astype(jnp.float32)
            square_sum += jnp.sum(features * features, axis=-1, keepdims=True)
        factor = lax.rsqrt(square_sum / depth + EPSILON)
        for part in range(section_count):
            cols = pl.ds(part * width, width)
            normed_ref[rows_of(place, capacity), cols] = (
                rows_all[part, place].astype(jnp.float32) * factor * gain_ref[:, cols]
            ).astype(jnp.bfloat16)

    tile = tile_spots * chip_rows
    total = seq_count * capacity
    lane = lax.broadcasted_iota(jnp.int32, (1, tile), 1)

    def fill_slots(index):
        key_slot = lane + index * tile
        for piece in range(tile // BLOCK):
            place = index * (tile // BLOCK) + piece
            within = lax.rem(place, slots)
            count = jnp.full((1, tile), count_ref[place // slots], jnp.int32)
            key_slot = jnp.where((lane // BLOCK == piece) & (count <= within), total, key_slot)
        key_slots[pl.ds(index, 1), :] = key_slot

    bundle = min(ratio, heads_half)
    bundles = heads_half // bundle
    scale = HEAD_DIM ** (-0.5)

    def fold(who, index):
        tall = lax.broadcasted_iota(jnp.int32, (bundle * chip_rows, 1), 0)
        query_slot = lax.rem(tall, chip_rows) + spots[who] * chip_rows
        key_slot = key_slots[pl.ds(index, 1), :]
        rows = rows_of(index, tile)
        for number in range(bundles):
            if kv_cols == HEAD_DIM:
                cols = pl.ds(0, HEAD_DIM)
            else:
                cols = rows_of((core * heads_half + number * bundle) // ratio, HEAD_DIM)
            keys = panel[0, rows, cols]
            values = panel[1, rows, cols]
            wide = queries_ref[who, pl.ds(number * bundle, bundle)].reshape(
                bundle * chip_rows, HEAD_DIM
            )
            scores = (
                lax.dot_general(
                    wide, keys, (((1,), (1,)), ((), ())), preferred_element_type=jnp.float32
                )
                * scale
            )
            weights = jnp.where(key_slot <= query_slot, jnp.exp(scores), 0.0)
            denom_ref[who, number] += jnp.sum(weights, axis=-1, keepdims=True)
            numer_ref[who, number] += jnp.dot(
                weights.astype(jnp.bfloat16), values, preferred_element_type=jnp.float32
            )

    def settle(who):
        for number in range(bundles):
            denom = denom_ref[who, number]
            safe = jnp.where(denom > 0, denom, 1.0)
            result = (numer_ref[who, number] / safe).astype(jnp.bfloat16)
            for head in range(bundle):
                cols = pl.ds((number * bundle + head) * HEAD_DIM, HEAD_DIM)
                heads_all[section, core, who, :, cols] = result[
                    head * chip_rows : (head + 1) * chip_rows
                ]

    def finish(part):
        update = jnp.zeros((2 * chip_rows, part_o), jnp.float32)
        for source in range(section_count):
            for half in range(2):
                update += jnp.dot(
                    heads_all[source, half].reshape(2 * chip_rows, half_q),
                    wo[part, pl.ds((source * 2 + half) * half_q, half_q), :],
                    preferred_element_type=jnp.float32,
                )
        cols = pl.ds(pl.multiple_of(core * half_o + part * part_o, part_o), part_o)

        def settle_rows(who):
            for half in range(2):
                place = who * 2 + half
                results[place, part] = (
                    rows_all[section, place, :, cols].astype(jnp.float32)
                    + gate_column(place) * update[place * capacity : (place + 1) * capacity]
                ).astype(out_ref.dtype)
                target = spots[who] * 2 + half
                pl.when(target != me)(lambda: give_back(place, part, target).start())

        pl.when(has_guest)(lambda: settle_rows(1))
        settle_rows(0)

    @pl.when(active)
    def _():
        others(lambda offset, peer: rows_spread(0, offset, peer).start())
        send_weight(KV)
        rows_to_pair(0, section).start()
        gate_copy(core).start()
        send_weight(QUERY)

        @pl.when(has_guest)
        def _():
            await_rows(section, 2 + core)
            others(lambda offset, peer: rows_spread(1, offset, peer).start())
            rows_to_pair(1, section).start()

        repeat(0, line // tile_spots, fill_slots)
        numer_ref[...] = jnp.zeros_like(numer_ref)
        denom_ref[...] = jnp.zeros_like(denom_ref)

        def gather(who):
            def forward(offset, peer):
                await_rows(peer, who * 2 + core)
                rows_to_pair(who, peer).start()

            others(forward)
            normalise(who * 2 + core)
            for part in range(section_count):
                await_rows(part, who * 2 + 1 - core)
            normalise(who * 2 + 1 - core)

        for_who(gather)
        await_weight(KV)
        sums = jnp.dot(normed_ref[...], wkv[...], preferred_element_type=jnp.float32).astype(
            jnp.bfloat16
        )

        def offer(who):
            panel[core, rows_of(spots[who], chip_rows), :] = sums[
                who * chip_rows : (who + 1) * chip_rows
            ]
            panel_to_pair(spots[who]).start()
            later_hosts(lambda host: panel_onward(who, host).start())

        for_who(offer)
        send_weight(OUT_A)
        send_weight(OUT_B)
        await_weight(QUERY)
        sums = jnp.dot(normed_ref[...], wq[...], preferred_element_type=jnp.float32).astype(
            jnp.bfloat16
        )
        for who in range(2):
            for head in range(heads_half):
                queries_ref[who, head] = sums[
                    who * chip_rows : (who + 1) * chip_rows,
                    head * HEAD_DIM : (head + 1) * HEAD_DIM,
                ]
        for_who(lambda who: await_panel(1 - core, spots[who]))
        for_who(lambda who: fold(who, spots[who] // tile_spots))

        def relay(place):
            await_panel(core, place)
            panel_to_pair(place).start()

        earlier_spots(relay)
        earlier_spots(lambda place: await_panel(1 - core, place))

        def rest(who):
            def body(index, carry):
                fold(who, index)
                return carry

            lax.fori_loop(0, spots[who] // tile_spots, body, 0)
            settle(who)
            others(lambda offset, peer: heads_spread(who, offset, peer).start())
            heads_to_pair(who, section).start()

        for_who(rest)

        def pass_on(who):
            def forward(offset, peer):
                await_heads(who, core, peer)
                heads_to_pair(who, peer).start()

            others(forward)

        for_who(pass_on)

        def collect(who):
            for part in range(section_count):
                await_heads(who, 1 - core, part)

        for_who(collect)
        gate_copy(1 - core).wait_recv()

        @pl.when(has_guest)
        def _():
            for half in range(2):
                gate_copy(2 + half).wait_recv()

        for part in range(2):
            await_weight(OUT_A + part)
            finish(part)

        def drain(who):
            others(lambda offset, peer: rows_spread(who, offset, peer).wait_send())
            others(lambda offset, peer: heads_spread(who, offset, peer).wait_send())
            for part in range(section_count):
                rows_to_pair(who, part).wait_send()
                heads_to_pair(who, part).wait_send()
            panel_to_pair(spots[who]).wait_send()
            later_hosts(lambda host: panel_onward(who, host).wait_send())
            for half in range(2):
                target = spots[who] * 2 + half
                for part in range(2):
                    pl.when(target != me)(
                        lambda: give_back(who * 2 + half, part, target).wait_send()
                    )

        for_who(drain)
        gate_copy(core).wait_send()
        earlier_spots(lambda place: panel_to_pair(place).wait_send())
        for part in range(2):
            for half in range(2):
                cols = pl.ds(half * half_o + part * part_o, part_o)

                @pl.when(core == half)
                def _():
                    out_ref[:, cols] = results[half, part]

                @pl.when(core != half)
                def _():
                    await_back(half, part)
                    out_ref[:, cols] = returned[half, part]

    for chunk in CHUNKS:
        finish_weight(chunk)

    @pl.when(jnp.logical_not(active))
    def _():
        for copy in guest_copies():
            copy.wait_send()
        for part in range(2):
            for half in range(2):
                await_back(half, part)
                cols = pl.ds(half * half_o + part * part_o, part_o)
                out_ref[:, cols] = returned[half, part]


def put(tokens_ref, rows_ref, chosen_ref, count_ref, mixed_ref):
    me = lax.axis_index("seq")
    mixed_ref[...] = tokens_ref[...]
    slots = rows_ref.shape[0] // BLOCK
    for slot in range(slots):

        @pl.when(slot < count_ref[me])
        def _():
            start = pl.multiple_of(chosen_ref[me * slots + slot] * BLOCK, BLOCK)
            mixed_ref[pl.ds(start, BLOCK), :] = rows_ref[slot * BLOCK : (slot + 1) * BLOCK, :]


def local(
    tokens, norm_gain, w_query, w_key, w_value, w_out, router_gate, chosen_blocks, block_counts
):
    seq_count = lax.axis_size("seq")
    section_count = lax.axis_size("section")
    tok_rows, width = tokens.shape
    slots = chosen_blocks.shape[1]
    capacity = slots * BLOCK
    chip_rows = 2 * capacity
    depth = section_count * width
    half_q = w_query.shape[1] // 2
    heads_half = half_q // HEAD_DIM
    part_o = w_out.shape[1] // 4
    kv_cols = w_key.shape[1]
    line = seq_count // 2
    tile_spots = 2 if line == 4 else 1
    tile = tile_spots * chip_rows
    bundle = min(HEADS // KV_HEADS, heads_half)

    vmem = pl.BlockSpec(memory_space=pltpu.VMEM)
    smem = pl.BlockSpec(memory_space=pltpu.SMEM)
    anywhere = pl.BlockSpec(memory_space=pl.ANY)
    bf16 = jnp.bfloat16
    dma = pltpu.SemaphoreType.DMA
    blocks = chosen_blocks.reshape(-1)
    new_rows = pl.pallas_call(
        functools.partial(kernel, seq_count, section_count, tile_spots),
        out_shape=jax.ShapeDtypeStruct((capacity, width), tokens.dtype),
        in_specs=[vmem] * 3 + [smem] * 2 + [anywhere] * 4,
        out_specs=vmem,
        scratch_shapes=[
            pltpu.VMEM((section_count, 4, capacity, width), bf16),
            pltpu.VMEM((4, slots, BLOCK), jnp.float32),
            pltpu.VMEM((4 * capacity, depth), bf16),
            pltpu.VMEM((depth, kv_cols), bf16),
            pltpu.VMEM((depth, half_q), bf16),
            pltpu.VMEM((2, w_out.shape[0] * seq_count, part_o), bf16),
            pltpu.VMEM((2, seq_count * capacity, kv_cols), bf16),
            pltpu.VMEM((2, heads_half, chip_rows, HEAD_DIM), bf16),
            pltpu.VMEM((2, heads_half // bundle, bundle * chip_rows, HEAD_DIM), jnp.float32),
            pltpu.VMEM((2, heads_half // bundle, bundle * chip_rows, 1), jnp.float32),
            pltpu.VMEM((section_count, 2, 2, chip_rows, half_q), bf16),
            pltpu.VMEM((4, 2, capacity, part_o), bf16),
            pltpu.VMEM((2, 2, capacity, part_o), bf16),
            pltpu.VMEM((line // tile_spots, tile), jnp.int32),
            dma((len(CHUNKS), seq_count)),
            dma((len(CHUNKS), seq_count)),
            dma((2, section_count)),
            dma((2, section_count)),
            dma((4, section_count)),
            dma((2,)),
            dma((4,)),
            dma((2, line)),
            dma((line,)),
            dma((2, line)),
            dma((2, section_count)),
            dma((2, section_count)),
            dma((2, 2, section_count)),
            dma((4, 2)),
            dma((2, 2)),
        ],
        compiler_params=pltpu.CompilerParams(collective_id=0, has_side_effects=True),
    )(
        tokens,
        norm_gain[None, :],
        router_gate.reshape(tok_rows // BLOCK, BLOCK),
        blocks,
        block_counts,
        w_query,
        w_key,
        w_value,
        w_out,
    )
    return pl.pallas_call(
        put,
        out_shape=jax.ShapeDtypeStruct(tokens.shape, tokens.dtype),
        in_specs=[vmem, vmem, smem, smem],
        out_specs=vmem,
    )(tokens, new_rows, blocks, block_counts)


def solution(mesh):
    return jax.shard_map(
        local,
        mesh=mesh,
        in_specs=(
            P("seq", "section"),
            P(),
            P("seq", "section"),
            P("seq", "section"),
            P("seq", "section"),
            P("seq", "section"),
            P("seq"),
            P(),
            P(),
        ),
        out_specs=P("seq", "section"),
        check_vma=False,
    )
```

```python
import functools

import jax
import jax.numpy as jnp
from jax import lax
from jax.experimental import pallas as pl
from jax.experimental.pallas import tpu as pltpu
from jax.sharding import PartitionSpec as P

HEADS = 16
KV_HEADS = 4
HEAD_DIM = 128
BLOCK = 128
EPSILON = 1e-05
MESH = pl.DeviceIdType.MESH

KV, QUERY, OUT = range(3)


def repeat(low, high, body):
    if high - low <= 8:
        for step in range(low, high):
            body(step)
    else:

        def wrapped(step, carry):
            body(step)
            return carry

        lax.fori_loop(low, high, wrapped, 0)


def kernel(
    seq_count,
    section_count,
    tile_spots,
    tokens_hbm,
    gain_ref,
    gate_ref,
    chosen_ref,
    count_ref,
    wq_in,
    wk_in,
    wv_in,
    wo_in,
    out_ref,
    tokens_ref,
    rows_all,
    gate_rows,
    normed_ref,
    wkv,
    wq,
    wo,
    panel,
    queries_ref,
    numer_ref,
    denom_ref,
    heads_all,
    results,
    returned,
    key_slots,
    tokens_sem,
    weight_send,
    weight_recv,
    guest_send,
    rows_send,
    rows_pair,
    rows_recv,
    gate_send,
    gate_recv,
    panel_line,
    panel_pair,
    panel_recv,
    heads_send,
    heads_pair,
    heads_recv,
    back_send,
    back_recv,
):
    me = lax.axis_index("seq")
    section = lax.axis_index("section")
    line = seq_count // 2
    spot = me // 2
    core = lax.rem(me, 2)
    pair = spot * 2 + 1 - core
    slots = chosen_ref.shape[1] // seq_count
    capacity, width = out_ref.shape
    chip_rows = 2 * capacity
    host_rows = 2 * chip_rows
    kv_cols = wk_in.shape[1]
    ratio = HEADS // KV_HEADS
    half_q = wq_in.shape[1] // 2
    heads_half = half_q // HEAD_DIM
    half_o = wo_in.shape[1] // 2
    parts_o, _, part_o = wo.shape
    depth = section_count * width
    chunks = [(KV, 0)]
    chunks += [(QUERY, head) for head in range(heads_half)]
    chunks += [(OUT, part) for part in range(parts_o)]
    number_of = {chunk: number for number, chunk in enumerate(chunks)}
    first, last = 1, line - 2
    active = (spot >= first) & (spot <= last)
    has_guest = (spot == first) | (spot == last)
    near = jnp.where(spot * 2 < line, 1, -1)
    guest_spot = spot - near
    host_spot = spot + near
    spots = (spot, guest_spot)
    beside = section + 1 - 2 * lax.rem(section, 2)
    above = lax.rem(section + 2, section_count)
    across = section_count - 1 - section

    def for_who(body):
        body(0)
        pl.when(has_guest)(lambda: body(1))

    def host_of(place):
        if isinstance(place, int):
            return min(max(place, first), last)
        return jnp.clip(place, first, last)

    def rows_of(block, size):
        if isinstance(block, int):
            return pl.ds(block * size, size)
        return pl.ds(pl.multiple_of(block * size, size), size)

    def remote(src, dst, send, receive, **device):
        return pltpu.make_async_remote_copy(
            src_ref=src,
            dst_ref=dst,
            send_sem=send,
            recv_sem=receive,
            device_id=device,
            device_id_type=MESH,
        )

    def weight_from(chunk, half):
        kind, part = chunk
        if kind == KV:
            return (wk_in, wv_in)[half]
        if kind == QUERY:
            return wq_in.at[:, pl.ds(half * half_q + part * HEAD_DIM, HEAD_DIM)]
        return wo_in.at[:, pl.ds(half * half_o + part * part_o, part_o)]

    def weight_to(chunk, block):
        kind, part = chunk
        if kind == KV:
            return wkv.at[rows_of(block, wk_in.shape[0]), :]
        if kind == QUERY:
            return wq.at[part, rows_of(block, wq_in.shape[0]), :]
        return wo.at[part, rows_of(block, wo_in.shape[0]), :]

    def weight_copy(chunk, half, target):
        number = number_of[chunk]
        return remote(
            weight_from(chunk, half),
            weight_to(chunk, me),
            weight_send.at[number, target],
            weight_recv.at[number, me],
            seq=target,
        )

    def send_weight(chunk):
        def body(host):
            for half in range(2):
                target = host * 2 + half

                @pl.when(target != me)
                def _():
                    weight_copy(chunk, half, target).start()

                @pl.when(target == me)
                def _():
                    pltpu.make_async_copy(
                        weight_from(chunk, half),
                        weight_to(chunk, me),
                        weight_recv.at[number_of[chunk], me],
                    ).start()

        repeat(first, last + 1, body)

    def finish_weight(chunk):
        def body(host):
            for half in range(2):
                target = host * 2 + half

                @pl.when(target != me)
                def _():
                    weight_copy(chunk, half, target).wait_send()

        repeat(first, last + 1, body)

    def await_weight(chunk, low=0, high=seq_count):
        def body(block):
            piece = weight_to(chunk, block)
            pltpu.make_async_copy(piece, piece, weight_recv.at[number_of[chunk], block]).wait()

        repeat(low, high, body)

    class Gather:
        def __init__(self, piece, send, pair_send, receive):
            self.piece, self.send, self.pair_send, self.receive = piece, send, pair_send, receive

        def copy(self, part, half, send, **device):
            piece = self.piece(part, half)
            return remote(piece, piece, send, self.receive.at[part, half], **device)

        def await_part(self, part, half):
            self.copy(part, half, self.send.at[0], seq=pair).wait_recv()

        def to_pair(self, part, half):
            return self.copy(part, half, self.pair_send.at[part, half], seq=pair)

        def sends(self):
            return (
                self.copy(section, 0, self.send.at[0], section=beside),
                self.copy(section, 1, self.send.at[1], section=above),
                self.copy(section, 1, self.send.at[2], section=beside),
                self.copy(section, 0, self.send.at[3], section=above),
            )

        def passes(self):
            return (
                self.copy(beside, 0, self.send.at[4], section=above),
                self.copy(above, 1, self.send.at[5], section=beside),
            )

        def start(self, ready=False):
            if ready:
                self.await_part(section, 0)
                self.await_part(section, 1)
            for copy in self.sends():
                copy.start()
            for half in range(2):
                self.to_pair(section, half).start()

        def relay(self):
            for (part, half), onward in zip(((beside, 0), (above, 1)), self.passes()):
                self.await_part(part, half)
                onward.start()
                self.to_pair(part, half).start()

        def complete(self):
            for part, half in ((beside, 1), (above, 0), (across, 0), (across, 1)):
                self.await_part(part, half)
                self.to_pair(part, half).start()

        def drain(self):
            for copy in self.sends() + self.passes():
                copy.wait_send()
            for part in range(section_count):
                for half in range(2):
                    self.to_pair(part, half).wait_send()

    def await_from_pair(piece, receive):
        for part in range(section_count):
            for half in range(2):
                remote(
                    piece(part, half),
                    piece(part, half),
                    receive.at[part, half],
                    receive.at[part, half],
                    seq=pair,
                ).wait_recv()

    def rows_piece(place):
        return lambda part, half: rows_all.at[part, place, rows_of(half, capacity // 2), :]

    def rows_gather(who):
        place = who * 2 + core
        return Gather(
            rows_piece(place), rows_send.at[who], rows_pair.at[who], rows_recv.at[place]
        )

    def guest_copies():
        copies = []
        for half in range(2):
            rows = rows_of(half, capacity // 2)
            copies.append(
                remote(
                    rows_all.at[section, core, rows, :],
                    rows_all.at[section, 2 + core, rows, :],
                    guest_send.at[half],
                    rows_recv.at[2 + core, section, half],
                    seq=host_spot * 2 + core,
                )
            )
        for half in range(2):
            copies.append(
                remote(
                    gate_rows.at[core],
                    gate_rows.at[2 + core],
                    gate_send.at[half],
                    gate_recv.at[2 + core],
                    seq=host_spot * 2 + half,
                )
            )
        return copies

    def gate_copy(place):
        return remote(
            gate_rows.at[place], gate_rows.at[place], gate_send.at[0], gate_recv.at[place], seq=pair
        )

    def panel_copy(kind, place, send, target):
        piece = panel.at[kind, rows_of(place, chip_rows), :]
        return remote(piece, piece, send, panel_recv.at[kind, place], seq=target)

    def panel_to_pair(place):
        return panel_copy(core, place, panel_pair.at[place], pair)

    def panel_onward(who, host):
        return panel_copy(core, spots[who], panel_line.at[who, host], host * 2 + core)

    def later_hosts(body):
        def guarded(host):
            pl.when(host > spot)(lambda: body(host))

        repeat(first, last + 1, guarded)

    def await_panel(kind, place):
        panel_copy(kind, place, panel_pair.at[place], pair).wait_recv()

    def earlier_spots(body):
        def guarded(place):
            pl.when(host_of(place) < spot)(lambda: body(place))

        repeat(0, line, guarded)

    def heads_piece(half_core, head):
        return lambda part, half: heads_all.at[part, half_core, head, rows_of(half, chip_rows), :]

    def heads_gather(head):
        return Gather(
            heads_piece(core, head),
            heads_send.at[head],
            heads_pair.at[head],
            heads_recv.at[head, core],
        )

    def give_back(place, part, target):
        return remote(
            results.at[place, part],
            returned.at[core, part],
            back_send.at[place, part],
            back_recv.at[core, part],
            seq=target,
        )

    def await_back(half, part):
        remote(
            returned.at[half, part],
            returned.at[half, part],
            back_send.at[0, part],
            back_recv.at[half, part],
            seq=pair,
        ).wait_recv()

    barrier = pltpu.get_barrier_semaphore()
    load_tokens = pltpu.make_async_copy(tokens_hbm, tokens_ref, tokens_sem.at[0])
    load_tokens.start()

    def greet(other):
        @pl.when((other != me) & (active | (other >= first * 2) & (other < (last + 1) * 2)))
        def _():
            pl.semaphore_signal(barrier, inc=1, device_id={"seq": other}, device_id_type=MESH)

    repeat(0, seq_count, greet)

    @pl.when(active)
    def _():
        for peer in (beside, above):
            pl.semaphore_signal(barrier, inc=1, device_id={"section": peer}, device_id_type=MESH)

    def pick(row_ref, index):
        row = row_ref[...]
        lane = lax.broadcasted_iota(jnp.int32, row.shape, 1)
        return jnp.sum(jnp.where(lane == index, row, 0), axis=1, keepdims=True)

    load_tokens.wait()
    for slot in range(slots):
        number = pick(chosen_ref, me * slots + slot)
        rows = tokens_ref[:BLOCK, :]
        gates = gate_ref[:1, :]
        for block in range(1, gate_ref.shape[0]):
            rows = jnp.where(
                jnp.broadcast_to(number, rows.shape) == block,
                tokens_ref[block * BLOCK : (block + 1) * BLOCK, :],
                rows,
            )
            gates = jnp.where(
                jnp.broadcast_to(number, gates.shape) == block,
                gate_ref[block : block + 1, :],
                gates,
            )
        rows_all[section, core, pl.ds(slot * BLOCK, BLOCK), :] = rows
        gate_rows[core, pl.ds(slot, 1), :] = gates

    hosts = (last - first + 1) * 2
    pl.semaphore_wait(barrier, jnp.where(active, seq_count - 1 + 2, hosts))

    @pl.when(jnp.logical_not(active))
    def _():
        for copy in guest_copies():
            copy.start()
        for chunk in chunks:
            send_weight(chunk)

    def gate_column(place):
        wide = gate_rows[place]
        square = lax.broadcasted_iota(jnp.int32, (BLOCK, BLOCK), 0) == lax.broadcasted_iota(
            jnp.int32, (BLOCK, BLOCK), 1
        )
        return jnp.concatenate(
            [
                jnp.sum(jnp.where(square, wide[slot : slot + 1, :], 0.0), axis=1, keepdims=True)
                for slot in range(slots)
            ],
            axis=0,
        )

    def normalise(place):
        square_sum = jnp.zeros((capacity, 1), jnp.float32)
        for part in range(section_count):
            features = rows_all[part, place].astype(jnp.float32)
            square_sum += jnp.sum(features * features, axis=-1, keepdims=True)
        factor = lax.rsqrt(square_sum / depth + EPSILON)
        for part in range(section_count):
            cols = pl.ds(part * width, width)
            normed_ref[rows_of(place, capacity), cols] = (
                rows_all[part, place].astype(jnp.float32) * factor * gain_ref[:, cols]
            ).astype(jnp.bfloat16)

    tile = tile_spots * chip_rows
    total = seq_count * capacity
    lane = lax.broadcasted_iota(jnp.int32, (1, tile), 1)

    def fill_slots(index):
        key_slot = lane + index * tile
        for piece in range(tile // BLOCK):
            place = index * (tile // BLOCK) + piece
            within = lax.rem(place, slots)
            count = jnp.broadcast_to(pick(count_ref, place // slots), (1, tile))
            key_slot = jnp.where((lane // BLOCK == piece) & (count <= within), total, key_slot)
        key_slots[pl.ds(index, 1), :] = key_slot

    scale = HEAD_DIM ** (-0.5)

    def fold(head, index):
        tall = lax.broadcasted_iota(jnp.int32, (host_rows, 1), 0)
        base = jnp.where(tall < chip_rows, spot * chip_rows, guest_spot * chip_rows - chip_rows)
        query_slot = tall + base
        key_slot = key_slots[pl.ds(index, 1), :]
        rows = rows_of(index, tile)
        if kv_cols == HEAD_DIM:
            cols = pl.ds(0, HEAD_DIM)
        else:
            cols = rows_of((core * heads_half + head) // ratio, HEAD_DIM)
        scores = (
            lax.dot_general(
                queries_ref[head],
                panel[0, rows, cols],
                (((1,), (1,)), ((), ())),
                preferred_element_type=jnp.float32,
            )
            * scale
        )
        weights = jnp.where(key_slot <= query_slot, jnp.exp(scores), 0.0)
        denom_ref[head] += jnp.sum(weights, axis=-1, keepdims=True)
        numer_ref[head] += jnp.dot(
            weights.astype(jnp.bfloat16), panel[1, rows, cols], preferred_element_type=jnp.float32
        )

    def fold_range(head, low, high):
        def body(index, carry):
            fold(head, index)
            return carry

        lax.fori_loop(low, high, body, 0)

    def finish(part):
        update = jnp.zeros((host_rows, part_o), jnp.float32)
        blocks = half_q // wo_in.shape[0]
        for source in range(section_count):
            for half in range(2):
                number = source * 2 + half
                await_weight((OUT, part), number * blocks, (number + 1) * blocks)
                attended = jnp.concatenate(
                    [heads_all[source, half, head] for head in range(heads_half)], axis=-1
                )
                update += jnp.dot(
                    attended,
                    wo[part, pl.ds(number * half_q, half_q), :],
                    preferred_element_type=jnp.float32,
                )
        cols = pl.ds(pl.multiple_of(core * half_o + part * part_o, part_o), part_o)

        def settle_rows(who):
            for half in range(2):
                place = who * 2 + half
                results[place, part] = (
                    rows_all[section, place, :, cols].astype(jnp.float32)
                    + gate_column(place) * update[place * capacity : (place + 1) * capacity]
                ).astype(out_ref.dtype)
                target = spots[who] * 2 + half
                pl.when(target != me)(lambda: give_back(place, part, target).start())

        pl.when(has_guest)(lambda: settle_rows(1))
        settle_rows(0)

    @pl.when(active)
    def _():
        rows_gather(0).start()
        send_weight((KV, 0))
        gate_copy(core).start()
        send_weight((QUERY, 0))
        repeat(0, line // tile_spots, fill_slots)
        numer_ref[...] = jnp.zeros_like(numer_ref)
        denom_ref[...] = jnp.zeros_like(denom_ref)
        rows_gather(0).relay()
        pl.when(has_guest)(lambda: rows_gather(1).start(ready=True))
        rows_gather(0).complete()
        pl.when(has_guest)(lambda: rows_gather(1).relay())
        normalise(core)
        await_from_pair(rows_piece(1 - core), rows_recv.at[1 - core])
        normalise(1 - core)

        @pl.when(has_guest)
        def _():
            rows_gather(1).complete()
            normalise(2 + core)
            await_from_pair(rows_piece(3 - core), rows_recv.at[3 - core])
            normalise(3 - core)

        await_weight((KV, 0))
        sums = jnp.dot(normed_ref[...], wkv[...], preferred_element_type=jnp.float32).astype(
            jnp.bfloat16
        )

        def offer(who):
            panel[core, rows_of(spots[who], chip_rows), :] = sums[
                who * chip_rows : (who + 1) * chip_rows
            ]
            panel_to_pair(spots[who]).start()
            later_hosts(lambda host: panel_onward(who, host).start())

        for_who(offer)
        for chunk in chunks[2:]:
            send_weight(chunk)
        own_tile = spot // tile_spots
        farthest = jnp.where(has_guest, jnp.maximum(spot, guest_spot), spot)
        tiles = farthest // tile_spots + 1
        for head in range(heads_half):
            await_weight((QUERY, head))
            queries_ref[head] = jnp.dot(
                normed_ref[...], wq[head], preferred_element_type=jnp.float32
            ).astype(jnp.bfloat16)
            if head == 0:
                for_who(lambda who: await_panel(1 - core, spots[who]))
            fold(head, own_tile)
            if head == 0:

                def pass_on(place):
                    await_panel(core, place)
                    panel_to_pair(place).start()

                earlier_spots(pass_on)
                earlier_spots(lambda place: await_panel(1 - core, place))
            fold_range(head, 0, own_tile)
            fold_range(head, own_tile + 1, tiles)
            denom = denom_ref[head]
            safe = jnp.where(denom > 0, denom, 1.0)
            heads_all[section, core, head] = (numer_ref[head] / safe).astype(jnp.bfloat16)
            heads_gather(head).start()
            heads_gather(head).relay()

        for head in range(heads_half):
            heads_gather(head).complete()
        for head in range(heads_half):
            await_from_pair(heads_piece(1 - core, head), heads_recv.at[head, 1 - core])
        gate_copy(1 - core).wait_recv()

        @pl.when(has_guest)
        def _():
            for half in range(2):
                gate_copy(2 + half).wait_recv()

        for part in range(parts_o):
            finish(part)

        def drain(who):
            rows_gather(who).drain()
            panel_to_pair(spots[who]).wait_send()
            later_hosts(lambda host: panel_onward(who, host).wait_send())
            for half in range(2):
                target = spots[who] * 2 + half
                for part in range(parts_o):
                    pl.when(target != me)(
                        lambda: give_back(who * 2 + half, part, target).wait_send()
                    )

        for_who(drain)
        for head in range(heads_half):
            heads_gather(head).drain()
        gate_copy(core).wait_send()
        earlier_spots(lambda place: panel_to_pair(place).wait_send())
        for part in range(parts_o):
            for half in range(2):
                cols = pl.ds(half * half_o + part * part_o, part_o)

                @pl.when(core == half)
                def _():
                    out_ref[:, cols] = results[half, part]

                @pl.when(core != half)
                def _():
                    await_back(half, part)
                    out_ref[:, cols] = returned[half, part]

    for chunk in chunks:
        finish_weight(chunk)

    @pl.when(jnp.logical_not(active))
    def _():
        for copy in guest_copies():
            copy.wait_send()
        for part in range(parts_o):
            for half in range(2):
                await_back(half, part)
                cols = pl.ds(half * half_o + part * part_o, part_o)
                out_ref[:, cols] = returned[half, part]


def put(tokens_ref, rows_ref, chosen_ref, count_ref, mixed_ref):
    me = lax.axis_index("seq")
    mixed_ref[...] = tokens_ref[...]
    slots = rows_ref.shape[0] // BLOCK
    for slot in range(slots):

        @pl.when(slot < count_ref[me])
        def _():
            start = pl.multiple_of(chosen_ref[me * slots + slot] * BLOCK, BLOCK)
            mixed_ref[pl.ds(start, BLOCK), :] = rows_ref[slot * BLOCK : (slot + 1) * BLOCK, :]


def local(
    tokens, norm_gain, w_query, w_key, w_value, w_out, router_gate, chosen_blocks, block_counts
):
    seq_count = lax.axis_size("seq")
    section_count = lax.axis_size("section")
    tok_rows, width = tokens.shape
    slots = chosen_blocks.shape[1]
    capacity = slots * BLOCK
    host_rows = 4 * capacity
    depth = section_count * width
    heads_half = w_query.shape[1] // 2 // HEAD_DIM
    parts_o = 2
    part_o = w_out.shape[1] // 2 // parts_o
    kv_cols = w_key.shape[1]
    line = seq_count // 2
    tile_spots = 2 if line == 4 else 1
    tile = tile_spots * 2 * capacity
    chunk_count = 1 + heads_half + parts_o

    vmem = pl.BlockSpec(memory_space=pltpu.VMEM)
    smem = pl.BlockSpec(memory_space=pltpu.SMEM)
    anywhere = pl.BlockSpec(memory_space=pl.ANY)
    bf16 = jnp.bfloat16
    f32 = jnp.float32
    dma = pltpu.SemaphoreType.DMA
    blocks = chosen_blocks.reshape(-1)
    new_rows = pl.pallas_call(
        functools.partial(kernel, seq_count, section_count, tile_spots),
        out_shape=jax.ShapeDtypeStruct((capacity, width), tokens.dtype),
        in_specs=[anywhere] + [vmem] * 4 + [anywhere] * 4,
        out_specs=vmem,
        scratch_shapes=[
            pltpu.VMEM(tokens.shape, bf16),
            pltpu.VMEM((section_count, 4, capacity, width), bf16),
            pltpu.VMEM((4, slots, BLOCK), f32),
            pltpu.VMEM((host_rows, depth), bf16),
            pltpu.VMEM((depth, kv_cols), bf16),
            pltpu.VMEM((heads_half, depth, HEAD_DIM), bf16),
            pltpu.VMEM((parts_o, w_out.shape[0] * seq_count, part_o), bf16),
            pltpu.VMEM((2, seq_count * capacity, kv_cols), bf16),
            pltpu.VMEM((heads_half, host_rows, HEAD_DIM), bf16),
            pltpu.VMEM((heads_half, host_rows, HEAD_DIM), f32),
            pltpu.VMEM((heads_half, host_rows, 1), f32),
            pltpu.VMEM((section_count, 2, heads_half, host_rows, HEAD_DIM), bf16),
            pltpu.VMEM((4, parts_o, capacity, part_o), bf16),
            pltpu.VMEM((2, parts_o, capacity, part_o), bf16),
            pltpu.VMEM((line // tile_spots, tile), jnp.int32),
            dma((1,)),
            dma((chunk_count, seq_count)),
            dma((chunk_count, seq_count)),
            dma((2,)),
            dma((2, 6)),
            dma((2, section_count, 2)),
            dma((4, section_count, 2)),
            dma((2,)),
            dma((4,)),
            dma((2, line)),
            dma((line,)),
            dma((2, line)),
            dma((heads_half, 6)),
            dma((heads_half, section_count, 2)),
            dma((heads_half, 2, section_count, 2)),
            dma((4, parts_o)),
            dma((2, parts_o)),
        ],
        compiler_params=pltpu.CompilerParams(collective_id=0, has_side_effects=True),
    )(
        tokens,
        norm_gain[None, :],
        router_gate.reshape(tok_rows // BLOCK, BLOCK),
        blocks[None, :],
        block_counts[None, :],
        w_query,
        w_key,
        w_value,
        w_out,
    )
    return pl.pallas_call(
        put,
        out_shape=jax.ShapeDtypeStruct(tokens.shape, tokens.dtype),
        in_specs=[vmem, vmem, smem, smem],
        out_specs=vmem,
    )(tokens, new_rows, blocks, block_counts)


def solution(mesh):
    return jax.shard_map(
        local,
        mesh=mesh,
        in_specs=(
            P("seq", "section"),
            P(),
            P("seq", "section"),
            P("seq", "section"),
            P("seq", "section"),
            P("seq", "section"),
            P("seq"),
            P(),
            P(),
        ),
        out_specs=P("seq", "section"),
        check_vma=False,
    )
```

```python
import functools

import jax
import jax.numpy as jnp
from jax import lax
from jax.experimental import pallas as pl
from jax.experimental.pallas import tpu as pltpu
from jax.sharding import PartitionSpec as P

HEADS = 16
KV_HEADS = 4
HEAD_DIM = 128
BLOCK = 128
EPSILON = 1e-05
MESH = pl.DeviceIdType.MESH

KV, QUERY, OUT = range(3)


def chunks_of(heads_half, parts_o):
    chunks = [(KV, 0)]
    chunks += [(QUERY, head) for head in range(heads_half)]
    chunks += [(OUT, part) for part in range(parts_o)]
    return chunks


def repeat(low, high, body):
    if high - low <= 8:
        for step in range(low, high):
            body(step)
    else:

        def wrapped(step, carry):
            body(step)
            return carry

        lax.fori_loop(low, high, wrapped, 0)


def kernel(
    seq_count,
    section_count,
    tile_spots,
    tokens_hbm,
    gain_ref,
    gate_ref,
    chosen_ref,
    count_ref,
    wq_in,
    wk_in,
    wv_in,
    wo_in,
    mixed_ref,
    out_ref,
    rows_all,
    gate_rows,
    normed_ref,
    wkv,
    wq,
    wo,
    panel,
    queries_ref,
    numer_ref,
    denom_ref,
    heads_all,
    results,
    returned,
    key_slots,
    tokens_sem,
    weight_send,
    weight_recv,
    guest_send,
    rows_send,
    rows_recv,
    gate_send,
    gate_recv,
    panel_line,
    panel_pair,
    panel_recv,
    heads_send,
    heads_recv,
    back_send,
    back_recv,
):
    me = lax.axis_index("seq")
    section = lax.axis_index("section")
    line = seq_count // 2
    spot = me // 2
    core = lax.rem(me, 2)
    pair = spot * 2 + 1 - core
    slots = chosen_ref.shape[1] // seq_count
    capacity, width = out_ref.shape
    chip_rows = 2 * capacity
    host_rows = 2 * chip_rows
    kv_cols = wk_in.shape[1]
    ratio = HEADS // KV_HEADS
    half_q = wq_in.shape[1] // 2
    heads_half = half_q // HEAD_DIM
    half_o = wo_in.shape[1] // 2
    parts_o, _, _, part_o = wo.shape
    depth = section_count * width
    chunks = chunks_of(heads_half, parts_o)
    number_of = {chunk: number for number, chunk in enumerate(chunks)}
    first, last = 1, line - 2
    hosts = last - first + 1
    active = (spot >= first) & (spot <= last)
    has_guest = (spot == first) | (spot == last)
    near = jnp.where(spot * 2 < line, 1, -1)
    guest_spot = spot - near
    host_spot = spot + near
    spots = (spot, guest_spot)
    beside = section + 1 - 2 * lax.rem(section, 2)
    above = lax.rem(section + 2, section_count)
    across = section_count - 1 - section

    def host_of(place):
        if isinstance(place, int):
            return min(max(place, first), last)
        return jnp.clip(place, first, last)

    def rows_of(block, size):
        if isinstance(block, int):
            return pl.ds(block * size, size)
        return pl.ds(pl.multiple_of(block * size, size), size)

    def remote(src, dst, send, receive, **device):
        return pltpu.make_async_remote_copy(
            src_ref=src,
            dst_ref=dst,
            send_sem=send,
            recv_sem=receive,
            device_id=device,
            device_id_type=MESH,
        )

    def await_bytes(ref, sem):
        pltpu.make_async_copy(ref, ref, sem).wait()

    def weight_from(chunk, half):
        kind, part = chunk
        if kind == KV:
            return (wk_in, wv_in)[half]
        if kind == QUERY:
            return wq_in.at[:, pl.ds(half * half_q + part * HEAD_DIM, HEAD_DIM)]
        return wo_in.at[:, pl.ds(half * half_o + part * part_o, part_o)]

    def weight_to(chunk, low, count):
        kind, part = chunk
        blocks = pl.ds(low, count)
        if kind == KV:
            return wkv.at[blocks]
        if kind == QUERY:
            return wq.at[part, blocks]
        return wo.at[part, blocks]

    def weight_copy(chunk, half, target):
        number = number_of[chunk]
        return remote(
            weight_from(chunk, half),
            weight_to(chunk, me, 1).at[0],
            weight_send.at[number],
            weight_recv.at[number],
            seq=target,
        )

    def send_weight(chunk):
        def body(host):
            for half in range(2):
                target = host * 2 + half

                @pl.when(target != me)
                def _():
                    weight_copy(chunk, half, target).start()

                @pl.when(target == me)
                def _():
                    pltpu.make_async_copy(
                        weight_from(chunk, half),
                        weight_to(chunk, me, 1).at[0],
                        weight_recv.at[number_of[chunk]],
                    ).start()

        repeat(first, last + 1, body)

    def receive_weight(chunk):
        await_bytes(weight_to(chunk, 0, seq_count), weight_recv.at[number_of[chunk]])

    def finish_weight(chunk, count):
        await_bytes(weight_to(chunk, 0, count), weight_send.at[number_of[chunk]])

    class Gather:
        def __init__(self, at, place, other, rows, send, receive):
            self.at, self.place, self.other, self.rows = at, place, other, rows
            self.send, self.receive = send, receive

        def copy(self, part, half, send, receive, **device):
            piece = self.at(pl.ds(part, 1), self.place).at[0].at[rows_of(half, self.rows)]
            return remote(piece, piece, send, receive, **device)

        def send_part(self, part, half, peer):
            receive = self.receive.at[part * 2 + half]
            self.copy(part, half, self.send.at[0], receive, section=peer).start()

        def await_part(self, part, half):
            receive = self.receive.at[part * 2 + half]
            self.copy(part, half, self.send.at[0], receive, seq=pair).wait_recv()

        def to_pair(self, part, half):
            receive = self.receive.at[section_count * 2]
            self.copy(part, half, self.send.at[1], receive, seq=pair).start()

        def start(self, ready=False):
            if ready:
                self.await_part(section, 0)
            self.send_part(section, 0, beside)
            if ready:
                self.await_part(section, 1)
            self.send_part(section, 1, above)
            self.send_part(section, 1, beside)
            self.send_part(section, 0, above)
            self.to_pair(section, 0)
            self.to_pair(section, 1)

        def relay(self):
            self.await_part(beside, 0)
            self.send_part(beside, 0, above)
            self.to_pair(beside, 0)
            self.await_part(above, 1)
            self.send_part(above, 1, beside)
            self.to_pair(above, 1)

        def near(self):
            for part, half in ((beside, 1), (above, 0)):
                self.await_part(part, half)
                self.to_pair(part, half)

        def far(self):
            for half in range(2):
                self.await_part(across, half)
                self.to_pair(across, half)

        def await_pair(self):
            everything = self.at(pl.ds(0, section_count), self.other)
            await_bytes(everything, self.receive.at[section_count * 2])

        def drain(self):
            await_bytes(self.at(pl.ds(0, 3), self.place), self.send.at[0])
            await_bytes(self.at(pl.ds(0, section_count), self.place), self.send.at[1])

    def rows_gather(who):
        return Gather(
            lambda parts, place: rows_all.at[place, parts],
            who * 2 + core,
            who * 2 + 1 - core,
            capacity // 2,
            rows_send.at[who],
            rows_recv.at[who],
        )

    def guest_copies():
        copies = []
        for half in range(2):
            rows = rows_of(half, capacity // 2)
            copies.append(
                remote(
                    rows_all.at[core, section, rows, :],
                    rows_all.at[2 + core, section, rows, :],
                    guest_send.at[0],
                    rows_recv.at[1, section * 2 + half],
                    seq=host_spot * 2 + core,
                )
            )
        for half in range(2):
            copies.append(
                remote(
                    gate_rows.at[core],
                    gate_rows.at[2 + core],
                    gate_send.at[0],
                    gate_recv.at[1],
                    seq=host_spot * 2 + half,
                )
            )
        return copies

    def gate_copy(place):
        return remote(
            gate_rows.at[place], gate_rows.at[place], gate_send.at[0], gate_recv.at[0], seq=pair
        )

    def panel_copy(kind, place, send, target):
        piece = panel.at[kind, rows_of(place, chip_rows), :]
        return remote(piece, piece, send, panel_recv.at[kind, place], seq=target)

    def panel_to_pair(place):
        return panel_copy(core, place, panel_pair.at[place], pair)

    def panel_onward(who, host):
        return panel_copy(core, spots[who], panel_line.at[who, host - first], host * 2 + core)

    def later_hosts(body):
        def guarded(host):
            pl.when(host > spot)(lambda: body(host))

        repeat(first + 1, last + 1, guarded)

    def await_panel(kind, place):
        panel_copy(kind, place, panel_pair.at[place], pair).wait_recv()

    def earlier_spots(body):
        def guarded(step):
            place = last - 1 - step
            pl.when(host_of(place) < spot)(lambda: body(place))

        repeat(0, last, guarded)

    def heads_gather(head):
        return Gather(
            lambda parts, place: heads_all.at[place, head, parts],
            core,
            1 - core,
            chip_rows,
            heads_send.at[head],
            heads_recv.at[head],
        )

    def give_back(place, part, target):
        return remote(
            results.at[place, part],
            returned.at[core, part],
            back_send.at[0],
            back_recv.at[part],
            seq=target,
        )

    barrier = pltpu.get_barrier_semaphore()
    load_tokens = pltpu.make_async_copy(tokens_hbm, mixed_ref, tokens_sem.at[0])
    load_tokens.start()

    def greet(other):
        @pl.when((other != me) & (active | (other >= first * 2) & (other < (last + 1) * 2)))
        def _():
            pl.semaphore_signal(barrier, inc=1, device_id={"seq": other}, device_id_type=MESH)

    repeat(0, seq_count, greet)

    @pl.when(active)
    def _():
        for peer in (beside, above):
            pl.semaphore_signal(barrier, inc=1, device_id={"section": peer}, device_id_type=MESH)

    def pick(row_ref, index):
        row = row_ref[...]
        lane = lax.broadcasted_iota(jnp.int32, row.shape, 1)
        return jnp.sum(jnp.where(lane == index, row, 0), axis=1, keepdims=True)

    load_tokens.wait()
    for slot in range(slots):
        number = pick(chosen_ref, me * slots + slot)
        rows = mixed_ref[:BLOCK, :]
        gates = gate_ref[:1, :]
        for block in range(1, gate_ref.shape[0]):
            rows = jnp.where(
                jnp.broadcast_to(number, rows.shape) == block,
                mixed_ref[block * BLOCK : (block + 1) * BLOCK, :],
                rows,
            )
            gates = jnp.where(
                jnp.broadcast_to(number, gates.shape) == block,
                gate_ref[block : block + 1, :],
                gates,
            )
        rows_all[core, section, pl.ds(slot * BLOCK, BLOCK), :] = rows
        gate_rows[core, pl.ds(slot, 1), :] = gates

    pl.semaphore_wait(barrier, jnp.where(active, seq_count - 1 + 2, hosts * 2))

    @pl.when(jnp.logical_not(active))
    def _():
        for copy in guest_copies():
            copy.start()
        for chunk in chunks:
            send_weight(chunk)

    def gate_column(place):
        wide = gate_rows[place]
        square = lax.broadcasted_iota(jnp.int32, (BLOCK, BLOCK), 0) == lax.broadcasted_iota(
            jnp.int32, (BLOCK, BLOCK), 1
        )
        return jnp.concatenate(
            [
                jnp.sum(jnp.where(square, wide[slot : slot + 1, :], 0.0), axis=1, keepdims=True)
                for slot in range(slots)
            ],
            axis=0,
        )

    def normalise(place):
        square_sum = jnp.zeros((capacity, 1), jnp.float32)
        for part in range(section_count):
            features = rows_all[place, part].astype(jnp.float32)
            square_sum += jnp.sum(features * features, axis=-1, keepdims=True)
        factor = lax.rsqrt(square_sum / depth + EPSILON)
        for part in range(section_count):
            cols = pl.ds(part * width, width)
            normed_ref[rows_of(place, capacity), cols] = (
                rows_all[place, part].astype(jnp.float32) * factor * gain_ref[:, cols]
            ).astype(jnp.bfloat16)

    tile = tile_spots * chip_rows
    total = seq_count * capacity
    lane = lax.broadcasted_iota(jnp.int32, (1, tile), 1)

    def fill_slots(index):
        key_slot = lane + index * tile
        for piece in range(tile // BLOCK):
            place = index * (tile // BLOCK) + piece
            within = lax.rem(place, slots)
            count = jnp.broadcast_to(pick(count_ref, place // slots), (1, tile))
            key_slot = jnp.where((lane // BLOCK == piece) & (count <= within), total, key_slot)
        key_slots[pl.ds(index, 1), :] = key_slot

    scale = HEAD_DIM ** (-0.5)

    def offer(who):
        panel[core, rows_of(spots[who], chip_rows), :] = jnp.dot(
            normed_ref[rows_of(who, chip_rows), :],
            wkv[...].reshape(depth, kv_cols),
            preferred_element_type=jnp.float32,
        ).astype(jnp.bfloat16)
        panel_to_pair(spots[who]).start()
        later_hosts(lambda host: panel_onward(who, host).start())

    def ask(head):
        for who in range(2):
            queries_ref[head, rows_of(who, chip_rows), :] = jnp.dot(
                normed_ref[rows_of(who, chip_rows), :],
                wq[head].reshape(depth, HEAD_DIM),
                preferred_element_type=jnp.float32,
            ).astype(jnp.bfloat16)

    def fold(head, index):
        tall = lax.broadcasted_iota(jnp.int32, (host_rows, 1), 0)
        base = jnp.where(tall < chip_rows, spot * chip_rows, guest_spot * chip_rows - chip_rows)
        query_slot = tall + base
        key_slot = key_slots[pl.ds(index, 1), :]
        rows = rows_of(index, tile)
        if kv_cols == HEAD_DIM:
            cols = pl.ds(0, HEAD_DIM)
        else:
            cols = rows_of((core * heads_half + head) // ratio, HEAD_DIM)
        scores = (
            lax.dot_general(
                queries_ref[head],
                panel[0, rows, cols],
                (((1,), (1,)), ((), ())),
                preferred_element_type=jnp.float32,
            )
            * scale
        )
        weights = jnp.where(key_slot <= query_slot, jnp.exp(scores), 0.0)
        denom_ref[head] += jnp.sum(weights, axis=-1, keepdims=True)
        numer_ref[head] += jnp.dot(
            weights.astype(jnp.bfloat16), panel[1, rows, cols], preferred_element_type=jnp.float32
        )

    def fold_range(head, low, high):
        def body(index, carry):
            fold(head, index)
            return carry

        lax.fori_loop(low, high, body, 0)

    def settle(head):
        denom = denom_ref[head]
        safe = jnp.where(denom > 0, denom, 1.0)
        heads_all[core, head, section] = (numer_ref[head] / safe).astype(jnp.bfloat16)

    def finish(who, part):
        attended = [
            heads_all[half, head, source, rows_of(who, chip_rows), :]
            for source in range(section_count)
            for half in range(2)
            for head in range(heads_half)
        ]
        update = jnp.dot(
            jnp.concatenate(attended, axis=-1),
            wo[part].reshape(-1, part_o),
            preferred_element_type=jnp.float32,
        )
        cols = pl.ds(pl.multiple_of(core * half_o + part * part_o, part_o), part_o)
        for half in range(2):
            place = who * 2 + half
            fresh = (
                rows_all[place, section, :, cols].astype(jnp.float32)
                + gate_column(place) * update[half * capacity : (half + 1) * capacity]
            ).astype(out_ref.dtype)
            target = spots[who] * 2 + half
            if who == 0:
                pl.when(target == me)(lambda: out_ref.__setitem__((slice(None), cols), fresh))

            @pl.when(target != me)
            def _():
                results[place, part] = fresh
                give_back(place, part, target).start()

    early = 2

    @pl.when(active)
    def _():
        rows_gather(0).start()
        for chunk in chunks[:early]:
            send_weight(chunk)

        @pl.when(spot == last)
        def _():
            for chunk in chunks[early:]:
                send_weight(chunk)

        gate_copy(core).start()
        repeat(0, line // tile_spots, fill_slots)
        numer_ref[...] = jnp.zeros_like(numer_ref)
        denom_ref[...] = jnp.zeros_like(denom_ref)
        rows_gather(0).relay()
        pl.when(has_guest)(lambda: rows_gather(1).start(ready=True))
        rows_gather(0).near()
        rows_gather(0).far()
        pl.when(has_guest)(lambda: rows_gather(1).relay())
        normalise(core)
        rows_gather(0).await_pair()
        normalise(1 - core)
        receive_weight(chunks[0])
        offer(0)
        @pl.when(has_guest)
        def _():
            rows_gather(1).near()
            rows_gather(1).far()
            normalise(2 + core)
            rows_gather(1).await_pair()
            normalise(3 - core)
            offer(1)

        @pl.when(spot != last)
        def _():
            for chunk in chunks[early:]:
                send_weight(chunk)

        own_tile = spot // tile_spots
        farthest = jnp.where(has_guest, jnp.maximum(spot, guest_spot), spot)
        tiles = farthest // tile_spots + 1
        for head in range(heads_half):
            receive_weight((QUERY, head))
            ask(head)
            if head == 0:
                await_panel(1 - core, spot)
                pl.when(has_guest)(lambda: await_panel(1 - core, guest_spot))
            fold(head, own_tile)
            if head == 0:

                def pass_on(place):
                    await_panel(core, place)
                    panel_to_pair(place).start()

                earlier_spots(pass_on)
                earlier_spots(lambda place: await_panel(1 - core, place))
            fold_range(head, 0, own_tile)
            fold_range(head, own_tile + 1, tiles)
            settle(head)
            heads_gather(head).start()
            if head > 0:
                heads_gather(head - 1).relay()

        heads_gather(heads_half - 1).relay()
        gate_copy(1 - core).wait_recv()
        pl.when(has_guest)(lambda: await_bytes(gate_rows.at[pl.ds(2, 2)], gate_recv.at[1]))
        for head in range(heads_half):
            heads_gather(head).near()
        for head in range(heads_half):
            heads_gather(head).far()
        for head in range(heads_half):
            heads_gather(head).await_pair()
        for part in range(parts_o):
            receive_weight((OUT, part))
            pl.when(has_guest)(lambda: finish(1, part))
            finish(0, part)

        rows_gather(0).drain()
        for head in range(heads_half):
            heads_gather(head).drain()
        await_bytes(gate_rows.at[pl.ds(0, 1)], gate_send.at[0])
        panel_to_pair(spot).wait_send()
        later_hosts(lambda host: panel_onward(0, host).wait_send())
        earlier_spots(lambda place: panel_to_pair(place).wait_send())

        @pl.when(has_guest)
        def _():
            rows_gather(1).drain()
            panel_to_pair(guest_spot).wait_send()
            later_hosts(lambda host: panel_onward(1, host).wait_send())
            await_bytes(results.at[pl.ds(0, 3)], back_send.at[0])

        @pl.when(jnp.logical_not(has_guest))
        def _():
            await_bytes(results.at[pl.ds(0, 1)], back_send.at[0])

        for chunk in chunks:
            finish_weight(chunk, hosts * 2 - 1)
        for part in range(parts_o):
            cols = pl.ds(pl.multiple_of((1 - core) * half_o + part * part_o, part_o), part_o)
            await_bytes(returned.at[1 - core, part], back_recv.at[part])
            out_ref[:, cols] = returned[1 - core, part]

    @pl.when(jnp.logical_not(active))
    def _():
        await_bytes(rows_all.at[core, section], guest_send.at[0])
        await_bytes(gate_rows.at[pl.ds(0, 2)], gate_send.at[0])
        for chunk in chunks:
            finish_weight(chunk, hosts * 2)
        for part in range(parts_o):
            await_bytes(returned.at[pl.ds(0, 2), part], back_recv.at[part])
            for half in range(2):
                cols = pl.ds(half * half_o + part * part_o, part_o)
                out_ref[:, cols] = returned[half, part]

    for slot in range(slots):
        number = pick(chosen_ref, me * slots + slot)
        count = pick(count_ref, me)
        number = jnp.where(count > slot, number, gate_ref.shape[0])
        fresh = out_ref[slot * BLOCK : (slot + 1) * BLOCK, :]
        for block in range(gate_ref.shape[0]):
            rows = pl.ds(block * BLOCK, BLOCK)
            mixed_ref[rows, :] = jnp.where(
                jnp.broadcast_to(number, fresh.shape) == block, fresh, mixed_ref[rows, :]
            )


def local(
    tokens, norm_gain, w_query, w_key, w_value, w_out, router_gate, chosen_blocks, block_counts
):
    seq_count = lax.axis_size("seq")
    section_count = lax.axis_size("section")
    tok_rows, width = tokens.shape
    slots = chosen_blocks.shape[1]
    capacity = slots * BLOCK
    host_rows = 4 * capacity
    depth = section_count * width
    heads_half = w_query.shape[1] // 2 // HEAD_DIM
    parts_o = 2
    part_o = w_out.shape[1] // 2 // parts_o
    kv_cols = w_key.shape[1]
    line = seq_count // 2
    tile_spots = 2 if line == 4 else 1
    tile = tile_spots * 2 * capacity
    chunk_count = len(chunks_of(heads_half, parts_o))

    vmem = pl.BlockSpec(memory_space=pltpu.VMEM)
    anywhere = pl.BlockSpec(memory_space=pl.ANY)
    bf16 = jnp.bfloat16
    f32 = jnp.float32
    dma = pltpu.SemaphoreType.DMA
    blocks = chosen_blocks.reshape(-1)
    return pl.pallas_call(
        functools.partial(kernel, seq_count, section_count, tile_spots),
        out_shape=pltpu.VMEM(tokens.shape, tokens.dtype),
        in_specs=[anywhere] + [vmem] * 4 + [anywhere] * 4,
        out_specs=vmem,
        scratch_shapes=[
            pltpu.VMEM((capacity, width), bf16),
            pltpu.VMEM((4, section_count, capacity, width), bf16),
            pltpu.VMEM((4, slots, BLOCK), f32),
            pltpu.VMEM((host_rows, depth), bf16),
            pltpu.VMEM((seq_count, w_key.shape[0], kv_cols), bf16),
            pltpu.VMEM((heads_half, seq_count, w_query.shape[0], HEAD_DIM), bf16),
            pltpu.VMEM((parts_o, seq_count, w_out.shape[0], part_o), bf16),
            pltpu.VMEM((2, seq_count * capacity, kv_cols), bf16),
            pltpu.VMEM((heads_half, host_rows, HEAD_DIM), bf16),
            pltpu.VMEM((heads_half, host_rows, HEAD_DIM), f32),
            pltpu.VMEM((heads_half, host_rows, 1), f32),
            pltpu.VMEM((2, heads_half, section_count, host_rows, HEAD_DIM), bf16),
            pltpu.VMEM((4, parts_o, capacity, part_o), bf16),
            pltpu.VMEM((2, parts_o, capacity, part_o), bf16),
            pltpu.VMEM((line // tile_spots, tile), jnp.int32),
            dma((1,)),
            dma((chunk_count,)),
            dma((chunk_count,)),
            dma((1,)),
            dma((2, 2)),
            dma((2, section_count * 2 + 1)),
            dma((1,)),
            dma((2,)),
            dma((2, line - 2)),
            dma((line,)),
            dma((2, line)),
            dma((heads_half, 2)),
            dma((heads_half, section_count * 2 + 1)),
            dma((1,)),
            dma((parts_o,)),
        ],
        compiler_params=pltpu.CompilerParams(collective_id=0, has_side_effects=True),
    )(
        tokens,
        norm_gain[None, :],
        router_gate.reshape(tok_rows // BLOCK, BLOCK),
        blocks[None, :],
        block_counts[None, :],
        w_query,
        w_key,
        w_value,
        w_out,
    )


def solution(mesh):
    return jax.shard_map(
        local,
        mesh=mesh,
        in_specs=(
            P("seq", "section"),
            P(),
            P("seq", "section"),
            P("seq", "section"),
            P("seq", "section"),
            P("seq", "section"),
            P("seq"),
            P(),
            P(),
        ),
        out_specs=P("seq", "section"),
        check_vma=False,
    )
```

```python
import functools

import jax
import jax.numpy as jnp
from jax import lax
from jax.experimental import pallas as pl
from jax.experimental.pallas import tpu as pltpu
from jax.sharding import PartitionSpec as P

HEADS = 16
KV_HEADS = 4
HEAD_DIM = 128
BLOCK = 128
EPSILON = 1e-05
MESH = pl.DeviceIdType.MESH

KV, QUERY, OUT = range(3)


def chunks_of(heads_half, parts_o):
    chunks = [(KV, 0)]
    chunks += [(QUERY, head) for head in range(heads_half)]
    chunks += [(OUT, part) for part in range(parts_o)]
    return chunks


def repeat(low, high, body):
    if high - low <= 8:
        for step in range(low, high):
            body(step)
    else:

        def wrapped(step, carry):
            body(step)
            return carry

        lax.fori_loop(low, high, wrapped, 0)


def kernel(
    seq_count,
    section_count,
    tile_spots,
    tokens_hbm,
    gain_hbm,
    gate_hbm,
    chosen_hbm,
    count_hbm,
    wq_in,
    wk_in,
    wv_in,
    wo_in,
    mixed_ref,
    gain_ref,
    gate_ref,
    chosen_ref,
    count_ref,
    out_ref,
    rows_all,
    gate_rows,
    normed_ref,
    wkv,
    wq,
    wo,
    panel,
    queries_ref,
    numer_ref,
    denom_ref,
    heads_all,
    results,
    returned,
    key_slots,
    load_sems,
    weight_send,
    weight_recv,
    guest_send,
    rows_send,
    rows_recv,
    gate_send,
    gate_recv,
    panel_line,
    panel_pair,
    panel_recv,
    heads_send,
    heads_recv,
    back_send,
    back_recv,
):
    me = lax.axis_index("seq")
    section = lax.axis_index("section")
    line = seq_count // 2
    spot = me // 2
    core = lax.rem(me, 2)
    pair = spot * 2 + 1 - core
    slots = chosen_ref.shape[1] // seq_count
    capacity, width = out_ref.shape
    chip_rows = 2 * capacity
    host_rows = 2 * chip_rows
    kv_cols = wk_in.shape[1]
    ratio = HEADS // KV_HEADS
    half_q = wq_in.shape[1] // 2
    heads_half = half_q // HEAD_DIM
    half_o = wo_in.shape[1] // 2
    parts_o, _, _, part_o = wo.shape
    depth = section_count * width
    chunks = chunks_of(heads_half, parts_o)
    number_of = {chunk: number for number, chunk in enumerate(chunks)}
    first, last = 1, line - 2
    hosts = last - first + 1
    active = (spot >= first) & (spot <= last)
    has_guest = (spot == first) | (spot == last)
    near = jnp.where(spot * 2 < line, 1, -1)
    guest_spot = spot - near
    host_spot = spot + near
    spots = (spot, guest_spot)
    beside = section + 1 - 2 * lax.rem(section, 2)
    above = lax.rem(section + 2, section_count)
    across = section_count - 1 - section

    def host_of(place):
        if isinstance(place, int):
            return min(max(place, first), last)
        return jnp.clip(place, first, last)

    def rows_of(block, size):
        if isinstance(block, int):
            return pl.ds(block * size, size)
        return pl.ds(pl.multiple_of(block * size, size), size)

    def remote(src, dst, send, receive, **device):
        return pltpu.make_async_remote_copy(
            src_ref=src,
            dst_ref=dst,
            send_sem=send,
            recv_sem=receive,
            device_id=device,
            device_id_type=MESH,
        )

    def await_bytes(ref, sem):
        pltpu.make_async_copy(ref, ref, sem).wait()

    def weight_from(chunk, half):
        kind, part = chunk
        if kind == KV:
            return (wk_in, wv_in)[half]
        if kind == QUERY:
            return wq_in.at[:, pl.ds(half * half_q + part * HEAD_DIM, HEAD_DIM)]
        return wo_in.at[:, pl.ds(half * half_o + part * part_o, part_o)]

    def weight_to(chunk, low, count):
        kind, part = chunk
        blocks = pl.ds(low, count)
        if kind == KV:
            return wkv.at[blocks]
        if kind == QUERY:
            return wq.at[part, blocks]
        return wo.at[part, blocks]

    def weight_copy(chunk, half, target):
        number = number_of[chunk]
        return remote(
            weight_from(chunk, half),
            weight_to(chunk, me, 1).at[0],
            weight_send.at[number],
            weight_recv.at[number],
            seq=target,
        )

    def send_weight(chunk):
        def body(host):
            for half in range(2):
                target = host * 2 + half

                @pl.when(target != me)
                def _():
                    weight_copy(chunk, half, target).start()

                @pl.when(target == me)
                def _():
                    pltpu.make_async_copy(
                        weight_from(chunk, half),
                        weight_to(chunk, me, 1).at[0],
                        weight_recv.at[number_of[chunk]],
                    ).start()

        repeat(first, last + 1, body)

    def receive_weight(chunk):
        await_bytes(weight_to(chunk, 0, seq_count), weight_recv.at[number_of[chunk]])

    def finish_weight(chunk, count):
        await_bytes(weight_to(chunk, 0, count), weight_send.at[number_of[chunk]])

    class Gather:
        def __init__(self, at, place, other, rows, send, receive):
            self.at, self.place, self.other, self.rows = at, place, other, rows
            self.send, self.receive = send, receive

        def copy(self, part, half, send, receive, **device):
            piece = self.at(pl.ds(part, 1), self.place).at[0].at[rows_of(half, self.rows)]
            return remote(piece, piece, send, receive, **device)

        def send_part(self, part, half, peer):
            receive = self.receive.at[part * 2 + half]
            self.copy(part, half, self.send.at[0], receive, section=peer).start()

        def await_part(self, part, half):
            receive = self.receive.at[part * 2 + half]
            self.copy(part, half, self.send.at[0], receive, seq=pair).wait_recv()

        def to_pair(self, part, half):
            receive = self.receive.at[section_count * 2]
            self.copy(part, half, self.send.at[1], receive, seq=pair).start()

        def start(self, ready=False):
            if ready:
                self.await_part(section, 0)
            self.send_part(section, 0, beside)
            if ready:
                self.await_part(section, 1)
            self.send_part(section, 1, above)
            self.send_part(section, 1, beside)
            self.send_part(section, 0, above)
            self.to_pair(section, 0)
            self.to_pair(section, 1)

        def relay(self):
            self.await_part(beside, 0)
            self.send_part(beside, 0, above)
            self.to_pair(beside, 0)
            self.await_part(above, 1)
            self.send_part(above, 1, beside)
            self.to_pair(above, 1)

        def near(self):
            for part, half in ((beside, 1), (above, 0)):
                self.await_part(part, half)
                self.to_pair(part, half)

        def far(self):
            for half in range(2):
                self.await_part(across, half)
                self.to_pair(across, half)

        def await_pair(self):
            everything = self.at(pl.ds(0, section_count), self.other)
            await_bytes(everything, self.receive.at[section_count * 2])

        def drain(self):
            await_bytes(self.at(pl.ds(0, 3), self.place), self.send.at[0])
            await_bytes(self.at(pl.ds(0, section_count), self.place), self.send.at[1])

    def rows_gather(who):
        return Gather(
            lambda parts, place: rows_all.at[place, parts],
            who * 2 + core,
            who * 2 + 1 - core,
            capacity // 2,
            rows_send.at[who],
            rows_recv.at[who],
        )

    def guest_copies():
        copies = []
        for half in range(2):
            rows = rows_of(half, capacity // 2)
            copies.append(
                remote(
                    rows_all.at[core, section, rows, :],
                    rows_all.at[2 + core, section, rows, :],
                    guest_send.at[0],
                    rows_recv.at[1, section * 2 + half],
                    seq=host_spot * 2 + core,
                )
            )
        for half in range(2):
            copies.append(
                remote(
                    gate_rows.at[core],
                    gate_rows.at[2 + core],
                    gate_send.at[0],
                    gate_recv.at[1],
                    seq=host_spot * 2 + half,
                )
            )
        return copies

    def gate_copy(place):
        return remote(
            gate_rows.at[place], gate_rows.at[place], gate_send.at[0], gate_recv.at[0], seq=pair
        )

    def panel_copy(kind, place, send, target):
        piece = panel.at[kind, rows_of(place, chip_rows), :]
        return remote(piece, piece, send, panel_recv.at[kind, place], seq=target)

    def panel_to_pair(place):
        return panel_copy(core, place, panel_pair.at[place], pair)

    def panel_onward(who, host):
        return panel_copy(core, spots[who], panel_line.at[who, host - first], host * 2 + core)

    def later_hosts(body):
        def guarded(host):
            pl.when(host > spot)(lambda: body(host))

        repeat(first + 1, last + 1, guarded)

    def await_panel(kind, place):
        panel_copy(kind, place, panel_pair.at[place], pair).wait_recv()

    def earlier_spots(body):
        def guarded(step):
            place = last - 1 - step
            pl.when(host_of(place) < spot)(lambda: body(place))

        repeat(0, last, guarded)

    def heads_gather(head):
        return Gather(
            lambda parts, place: heads_all.at[place, head, parts],
            core,
            1 - core,
            chip_rows,
            heads_send.at[head],
            heads_recv.at[head],
        )

    def give_back(place, part, target):
        return remote(
            results.at[place, part],
            returned.at[core, part],
            back_send.at[0],
            back_recv.at[part],
            seq=target,
        )

    barrier = pltpu.get_barrier_semaphore()
    loads = [
        pltpu.make_async_copy(source, target, load_sems.at[number])
        for number, (source, target) in enumerate(
            (
                (tokens_hbm, mixed_ref),
                (chosen_hbm, chosen_ref),
                (gate_hbm, gate_ref),
                (gain_hbm, gain_ref),
                (count_hbm, count_ref),
            )
        )
    ]
    for load in loads:
        load.start()

    def greet(other):
        @pl.when((other != me) & (active | (other >= first * 2) & (other < (last + 1) * 2)))
        def _():
            pl.semaphore_signal(barrier, inc=1, device_id={"seq": other}, device_id_type=MESH)

    repeat(0, seq_count, greet)

    @pl.when(active)
    def _():
        for peer in (beside, above):
            pl.semaphore_signal(barrier, inc=1, device_id={"section": peer}, device_id_type=MESH)

    def pick(row_ref, index):
        row = row_ref[...]
        lane = lax.broadcasted_iota(jnp.int32, row.shape, 1)
        return jnp.sum(jnp.where(lane == index, row, 0), axis=1, keepdims=True)

    for load in loads:
        load.wait()
    for slot in range(slots):
        number = pick(chosen_ref, me * slots + slot)
        rows = mixed_ref[:BLOCK, :]
        gates = gate_ref[:1, :]
        for block in range(1, gate_ref.shape[0]):
            rows = jnp.where(
                jnp.broadcast_to(number, rows.shape) == block,
                mixed_ref[block * BLOCK : (block + 1) * BLOCK, :],
                rows,
            )
            gates = jnp.where(
                jnp.broadcast_to(number, gates.shape) == block,
                gate_ref[block : block + 1, :],
                gates,
            )
        rows_all[core, section, pl.ds(slot * BLOCK, BLOCK), :] = rows
        gate_rows[core, pl.ds(slot, 1), :] = gates

    pl.semaphore_wait(barrier, jnp.where(active, seq_count - 1 + 2, hosts * 2))

    @pl.when(jnp.logical_not(active))
    def _():
        for copy in guest_copies():
            copy.start()
        for chunk in chunks:
            send_weight(chunk)

    def gate_column(place):
        wide = gate_rows[place]
        square = lax.broadcasted_iota(jnp.int32, (BLOCK, BLOCK), 0) == lax.broadcasted_iota(
            jnp.int32, (BLOCK, BLOCK), 1
        )
        return jnp.concatenate(
            [
                jnp.sum(jnp.where(square, wide[slot : slot + 1, :], 0.0), axis=1, keepdims=True)
                for slot in range(slots)
            ],
            axis=0,
        )

    def normalise(place):
        square_sum = jnp.zeros((capacity, 1), jnp.float32)
        for part in range(section_count):
            features = rows_all[place, part].astype(jnp.float32)
            square_sum += jnp.sum(features * features, axis=-1, keepdims=True)
        factor = lax.rsqrt(square_sum / depth + EPSILON)
        for part in range(section_count):
            cols = pl.ds(part * width, width)
            normed_ref[rows_of(place, capacity), cols] = (
                rows_all[place, part].astype(jnp.float32) * factor * gain_ref[:, cols]
            ).astype(jnp.bfloat16)

    tile = tile_spots * chip_rows
    total = seq_count * capacity
    lane = lax.broadcasted_iota(jnp.int32, (1, tile), 1)

    def fill_slots(index):
        key_slot = lane + index * tile
        for piece in range(tile // BLOCK):
            place = index * (tile // BLOCK) + piece
            within = lax.rem(place, slots)
            count = jnp.broadcast_to(pick(count_ref, place // slots), (1, tile))
            key_slot = jnp.where((lane // BLOCK == piece) & (count <= within), total, key_slot)
        key_slots[pl.ds(index, 1), :] = key_slot

    scale = HEAD_DIM ** (-0.5)

    def offer(who):
        panel[core, rows_of(spots[who], chip_rows), :] = jnp.dot(
            normed_ref[rows_of(who, chip_rows), :],
            wkv[...].reshape(depth, kv_cols),
            preferred_element_type=jnp.float32,
        ).astype(jnp.bfloat16)
        panel_to_pair(spots[who]).start()
        later_hosts(lambda host: panel_onward(who, host).start())

    def ask(head):
        for who in range(2):
            queries_ref[head, rows_of(who, chip_rows), :] = jnp.dot(
                normed_ref[rows_of(who, chip_rows), :],
                wq[head].reshape(depth, HEAD_DIM),
                preferred_element_type=jnp.float32,
            ).astype(jnp.bfloat16)

    def fold(head, index):
        tall = lax.broadcasted_iota(jnp.int32, (host_rows, 1), 0)
        base = jnp.where(tall < chip_rows, spot * chip_rows, guest_spot * chip_rows - chip_rows)
        query_slot = tall + base
        key_slot = key_slots[pl.ds(index, 1), :]
        rows = rows_of(index, tile)
        if kv_cols == HEAD_DIM:
            cols = pl.ds(0, HEAD_DIM)
        else:
            cols = rows_of((core * heads_half + head) // ratio, HEAD_DIM)
        scores = (
            lax.dot_general(
                queries_ref[head],
                panel[0, rows, cols],
                (((1,), (1,)), ((), ())),
                preferred_element_type=jnp.float32,
            )
            * scale
        )
        weights = jnp.where(key_slot <= query_slot, jnp.exp(scores), 0.0)
        denom_ref[head] += jnp.sum(weights, axis=-1, keepdims=True)
        numer_ref[head] += jnp.dot(
            weights.astype(jnp.bfloat16), panel[1, rows, cols], preferred_element_type=jnp.float32
        )

    def fold_range(head, low, high):
        def body(index, carry):
            fold(head, index)
            return carry

        lax.fori_loop(low, high, body, 0)

    def settle(head):
        denom = denom_ref[head]
        safe = jnp.where(denom > 0, denom, 1.0)
        heads_all[core, head, section] = (numer_ref[head] / safe).astype(jnp.bfloat16)

    def finish(who, part):
        attended = [
            heads_all[half, head, source, rows_of(who, chip_rows), :]
            for source in range(section_count)
            for half in range(2)
            for head in range(heads_half)
        ]
        update = jnp.dot(
            jnp.concatenate(attended, axis=-1),
            wo[part].reshape(-1, part_o),
            preferred_element_type=jnp.float32,
        )
        cols = pl.ds(pl.multiple_of(core * half_o + part * part_o, part_o), part_o)
        for half in range(2):
            place = who * 2 + half
            fresh = (
                rows_all[place, section, :, cols].astype(jnp.float32)
                + gate_column(place) * update[half * capacity : (half + 1) * capacity]
            ).astype(out_ref.dtype)
            target = spots[who] * 2 + half
            if who == 0:
                pl.when(target == me)(lambda: out_ref.__setitem__((slice(None), cols), fresh))

            @pl.when(target != me)
            def _():
                results[place, part] = fresh
                give_back(place, part, target).start()

    early = 2

    @pl.when(active)
    def _():
        rows_gather(0).start()
        for chunk in chunks[:early]:
            send_weight(chunk)

        @pl.when(spot == last)
        def _():
            for chunk in chunks[early:]:
                send_weight(chunk)

        gate_copy(core).start()
        repeat(0, line // tile_spots, fill_slots)
        numer_ref[...] = jnp.zeros_like(numer_ref)
        denom_ref[...] = jnp.zeros_like(denom_ref)
        rows_gather(0).relay()
        pl.when(has_guest)(lambda: rows_gather(1).start(ready=True))
        rows_gather(0).near()
        rows_gather(0).far()
        pl.when(has_guest)(lambda: rows_gather(1).relay())
        normalise(core)
        rows_gather(0).await_pair()
        normalise(1 - core)
        receive_weight(chunks[0])
        offer(0)
        @pl.when(has_guest)
        def _():
            rows_gather(1).near()
            rows_gather(1).far()
            normalise(2 + core)
            rows_gather(1).await_pair()
            normalise(3 - core)
            offer(1)

        @pl.when(spot != last)
        def _():
            for chunk in chunks[early:]:
                send_weight(chunk)

        own_tile = spot // tile_spots
        farthest = jnp.where(has_guest, jnp.maximum(spot, guest_spot), spot)
        tiles = farthest // tile_spots + 1
        for head in range(heads_half):
            receive_weight((QUERY, head))
            ask(head)
            if head == 0:
                await_panel(1 - core, spot)
                pl.when(has_guest)(lambda: await_panel(1 - core, guest_spot))
            fold(head, own_tile)
            if head == 0:

                def pass_on(place):
                    await_panel(core, place)
                    panel_to_pair(place).start()

                earlier_spots(pass_on)
                earlier_spots(lambda place: await_panel(1 - core, place))
            fold_range(head, 0, own_tile)
            fold_range(head, own_tile + 1, tiles)
            settle(head)
            heads_gather(head).start()
            if head > 0:
                heads_gather(head - 1).relay()

        heads_gather(heads_half - 1).relay()
        gate_copy(1 - core).wait_recv()
        pl.when(has_guest)(lambda: await_bytes(gate_rows.at[pl.ds(2, 2)], gate_recv.at[1]))
        for head in range(heads_half):
            heads_gather(head).near()
        for head in range(heads_half):
            heads_gather(head).far()
        for head in range(heads_half):
            heads_gather(head).await_pair()
        for part in range(parts_o):
            receive_weight((OUT, part))
            pl.when(has_guest)(lambda: finish(1, part))
            finish(0, part)

        rows_gather(0).drain()
        for head in range(heads_half):
            heads_gather(head).drain()
        await_bytes(gate_rows.at[pl.ds(0, 1)], gate_send.at[0])
        panel_to_pair(spot).wait_send()
        later_hosts(lambda host: panel_onward(0, host).wait_send())
        earlier_spots(lambda place: panel_to_pair(place).wait_send())

        @pl.when(has_guest)
        def _():
            rows_gather(1).drain()
            panel_to_pair(guest_spot).wait_send()
            later_hosts(lambda host: panel_onward(1, host).wait_send())
            await_bytes(results.at[pl.ds(0, 3)], back_send.at[0])

        @pl.when(jnp.logical_not(has_guest))
        def _():
            await_bytes(results.at[pl.ds(0, 1)], back_send.at[0])

        for chunk in chunks:
            finish_weight(chunk, hosts * 2 - 1)
        for part in range(parts_o):
            cols = pl.ds(pl.multiple_of((1 - core) * half_o + part * part_o, part_o), part_o)
            await_bytes(returned.at[1 - core, part], back_recv.at[part])
            out_ref[:, cols] = returned[1 - core, part]

    @pl.when(jnp.logical_not(active))
    def _():
        await_bytes(rows_all.at[core, section], guest_send.at[0])
        await_bytes(gate_rows.at[pl.ds(0, 2)], gate_send.at[0])
        for chunk in chunks:
            finish_weight(chunk, hosts * 2)
        for part in range(parts_o):
            await_bytes(returned.at[pl.ds(0, 2), part], back_recv.at[part])
            for half in range(2):
                cols = pl.ds(half * half_o + part * part_o, part_o)
                out_ref[:, cols] = returned[half, part]

    for slot in range(slots):
        number = pick(chosen_ref, me * slots + slot)
        count = pick(count_ref, me)
        number = jnp.where(count > slot, number, gate_ref.shape[0])
        fresh = out_ref[slot * BLOCK : (slot + 1) * BLOCK, :]
        for block in range(gate_ref.shape[0]):
            rows = pl.ds(block * BLOCK, BLOCK)
            mixed_ref[rows, :] = jnp.where(
                jnp.broadcast_to(number, fresh.shape) == block, fresh, mixed_ref[rows, :]
            )


def local(
    tokens, norm_gain, w_query, w_key, w_value, w_out, router_gate, chosen_blocks, block_counts
):
    seq_count = lax.axis_size("seq")
    section_count = lax.axis_size("section")
    tok_rows, width = tokens.shape
    slots = chosen_blocks.shape[1]
    capacity = slots * BLOCK
    host_rows = 4 * capacity
    depth = section_count * width
    heads_half = w_query.shape[1] // 2 // HEAD_DIM
    parts_o = 2
    part_o = w_out.shape[1] // 2 // parts_o
    kv_cols = w_key.shape[1]
    line = seq_count // 2
    tile_spots = 2 if line == 4 else 1
    tile = tile_spots * 2 * capacity
    chunk_count = len(chunks_of(heads_half, parts_o))

    vmem = pl.BlockSpec(memory_space=pltpu.VMEM)
    anywhere = pl.BlockSpec(memory_space=pl.ANY)
    bf16 = jnp.bfloat16
    f32 = jnp.float32
    dma = pltpu.SemaphoreType.DMA
    blocks = chosen_blocks.reshape(-1)
    return pl.pallas_call(
        functools.partial(kernel, seq_count, section_count, tile_spots),
        out_shape=pltpu.VMEM(tokens.shape, tokens.dtype),
        in_specs=[anywhere] * 9,
        out_specs=vmem,
        scratch_shapes=[
            pltpu.VMEM((1, depth), f32),
            pltpu.VMEM((tok_rows // BLOCK, BLOCK), f32),
            pltpu.VMEM((1, blocks.shape[0]), jnp.int32),
            pltpu.VMEM((1, seq_count), jnp.int32),
            pltpu.VMEM((capacity, width), bf16),
            pltpu.VMEM((4, section_count, capacity, width), bf16),
            pltpu.VMEM((4, slots, BLOCK), f32),
            pltpu.VMEM((host_rows, depth), bf16),
            pltpu.VMEM((seq_count, w_key.shape[0], kv_cols), bf16),
            pltpu.VMEM((heads_half, seq_count, w_query.shape[0], HEAD_DIM), bf16),
            pltpu.VMEM((parts_o, seq_count, w_out.shape[0], part_o), bf16),
            pltpu.VMEM((2, seq_count * capacity, kv_cols), bf16),
            pltpu.VMEM((heads_half, host_rows, HEAD_DIM), bf16),
            pltpu.VMEM((heads_half, host_rows, HEAD_DIM), f32),
            pltpu.VMEM((heads_half, host_rows, 1), f32),
            pltpu.VMEM((2, heads_half, section_count, host_rows, HEAD_DIM), bf16),
            pltpu.VMEM((4, parts_o, capacity, part_o), bf16),
            pltpu.VMEM((2, parts_o, capacity, part_o), bf16),
            pltpu.VMEM((line // tile_spots, tile), jnp.int32),
            dma((5,)),
            dma((chunk_count,)),
            dma((chunk_count,)),
            dma((1,)),
            dma((2, 2)),
            dma((2, section_count * 2 + 1)),
            dma((1,)),
            dma((2,)),
            dma((2, line - 2)),
            dma((line,)),
            dma((2, line)),
            dma((heads_half, 2)),
            dma((heads_half, section_count * 2 + 1)),
            dma((1,)),
            dma((parts_o,)),
        ],
        compiler_params=pltpu.CompilerParams(collective_id=0, has_side_effects=True),
    )(
        tokens,
        norm_gain[None, :],
        router_gate.reshape(tok_rows // BLOCK, BLOCK),
        blocks[None, :],
        block_counts[None, :],
        w_query,
        w_key,
        w_value,
        w_out,
    )


def solution(mesh):
    return jax.shard_map(
        local,
        mesh=mesh,
        in_specs=(
            P("seq", "section"),
            P(),
            P("seq", "section"),
            P("seq", "section"),
            P("seq", "section"),
            P("seq", "section"),
            P("seq"),
            P(),
            P(),
        ),
        out_specs=P("seq", "section"),
        check_vma=False,
    )
```

```python
import functools

import jax
import jax.numpy as jnp
from jax import lax
from jax.experimental import pallas as pl
from jax.experimental.pallas import tpu as pltpu
from jax.sharding import PartitionSpec as P

HEADS = 16
KV_HEADS = 4
HEAD_DIM = 128
BLOCK = 128
EPSILON = 1e-05
MESH = pl.DeviceIdType.MESH

KV, QUERY, OUT = range(3)


def chunks_of(heads_half, parts_o):
    chunks = [(KV, 0)]
    chunks += [(QUERY, head) for head in range(heads_half)]
    chunks += [(OUT, part) for part in range(parts_o)]
    return chunks


def repeat(low, high, body):
    if high - low <= 8:
        for step in range(low, high):
            body(step)
    else:

        def wrapped(step, carry):
            body(step)
            return carry

        lax.fori_loop(low, high, wrapped, 0)


def kernel(
    seq_count,
    section_count,
    tile_spots,
    tokens_hbm,
    gain_hbm,
    gate_hbm,
    chosen_hbm,
    count_hbm,
    wq_in,
    wk_in,
    wv_in,
    wo_in,
    mixed_ref,
    gain_ref,
    gate_ref,
    chosen_ref,
    count_ref,
    out_ref,
    rows_all,
    gate_rows,
    normed_ref,
    wkv,
    wq,
    wo,
    panel,
    queries_ref,
    numer_ref,
    denom_ref,
    heads_all,
    results,
    returned,
    key_slots,
    load_sems,
    weight_send,
    weight_recv,
    guest_send,
    rows_send,
    rows_recv,
    gate_send,
    gate_recv,
    panel_line,
    panel_pair,
    panel_recv,
    heads_send,
    heads_recv,
    back_send,
    back_recv,
):
    me = lax.axis_index("seq")
    section = lax.axis_index("section")
    line = seq_count // 2
    spot = me // 2
    core = lax.rem(me, 2)
    pair = spot * 2 + 1 - core
    slots = chosen_ref.shape[1] // seq_count
    capacity, width = out_ref.shape
    chip_rows = 2 * capacity
    host_rows = 2 * chip_rows
    kv_cols = wk_in.shape[1]
    ratio = HEADS // KV_HEADS
    half_q = wq_in.shape[1] // 2
    heads_half = half_q // HEAD_DIM
    half_o = wo_in.shape[1] // 2
    parts_o, _, _, part_o = wo.shape
    depth = section_count * width
    chunks = chunks_of(heads_half, parts_o)
    number_of = {chunk: number for number, chunk in enumerate(chunks)}
    first, last = 1, line - 2
    hosts = last - first + 1
    active = (spot >= first) & (spot <= last)
    has_guest = (spot == first) | (spot == last)
    near = jnp.where(spot * 2 < line, 1, -1)
    guest_spot = spot - near
    host_spot = spot + near
    spots = (spot, guest_spot)
    beside = section + 1 - 2 * lax.rem(section, 2)
    above = lax.rem(section + 2, section_count)
    across = section_count - 1 - section

    def host_of(place):
        if isinstance(place, int):
            return min(max(place, first), last)
        return jnp.clip(place, first, last)

    def rows_of(block, size):
        if isinstance(block, int):
            return pl.ds(block * size, size)
        return pl.ds(pl.multiple_of(block * size, size), size)

    def remote(src, dst, send, receive, **device):
        return pltpu.make_async_remote_copy(
            src_ref=src,
            dst_ref=dst,
            send_sem=send,
            recv_sem=receive,
            device_id=device,
            device_id_type=MESH,
        )

    def await_bytes(ref, sem):
        pltpu.make_async_copy(ref, ref, sem).wait()

    def weight_from(chunk, half):
        kind, part = chunk
        if kind == KV:
            return (wk_in, wv_in)[half]
        if kind == QUERY:
            return wq_in.at[:, pl.ds(half * half_q + part * HEAD_DIM, HEAD_DIM)]
        return wo_in.at[:, pl.ds(half * half_o + part * part_o, part_o)]

    def weight_to(chunk, low, count):
        kind, part = chunk
        blocks = pl.ds(low, count)
        if kind == KV:
            return wkv.at[blocks]
        if kind == QUERY:
            return wq.at[part, blocks]
        return wo.at[part, blocks]

    def weight_copy(chunk, half, target):
        number = number_of[chunk]
        return remote(
            weight_from(chunk, half),
            weight_to(chunk, me, 1).at[0],
            weight_send.at[number],
            weight_recv.at[number],
            seq=target,
        )

    def send_weight(chunk):
        def body(host):
            for half in range(2):
                target = host * 2 + half

                @pl.when(target != me)
                def _():
                    weight_copy(chunk, half, target).start()

                @pl.when(target == me)
                def _():
                    pltpu.make_async_copy(
                        weight_from(chunk, half),
                        weight_to(chunk, me, 1).at[0],
                        weight_recv.at[number_of[chunk]],
                    ).start()

        repeat(first, last + 1, body)

    def receive_weight(chunk):
        await_bytes(weight_to(chunk, 0, seq_count), weight_recv.at[number_of[chunk]])

    def finish_weight(chunk, count):
        await_bytes(weight_to(chunk, 0, count), weight_send.at[number_of[chunk]])

    class Gather:
        def __init__(self, at, place, other, rows, send, receive):
            self.at, self.place, self.other, self.rows = at, place, other, rows
            self.send, self.receive = send, receive

        def copy(self, part, half, send, receive, **device):
            piece = self.at(pl.ds(part, 1), self.place).at[0].at[rows_of(half, self.rows)]
            return remote(piece, piece, send, receive, **device)

        def send_part(self, part, half, peer):
            receive = self.receive.at[part * 2 + half]
            self.copy(part, half, self.send.at[0], receive, section=peer).start()

        def await_part(self, part, half):
            receive = self.receive.at[part * 2 + half]
            self.copy(part, half, self.send.at[0], receive, seq=pair).wait_recv()

        def to_pair(self, part, half):
            receive = self.receive.at[section_count * 2]
            self.copy(part, half, self.send.at[1], receive, seq=pair).start()

        def start(self, ready=False):
            if ready:
                self.await_part(section, 0)
            self.send_part(section, 0, beside)
            if ready:
                self.await_part(section, 1)
            self.send_part(section, 1, above)
            self.send_part(section, 1, beside)
            self.send_part(section, 0, above)
            self.to_pair(section, 0)
            self.to_pair(section, 1)

        def relay(self):
            self.await_part(beside, 0)
            self.send_part(beside, 0, above)
            self.to_pair(beside, 0)
            self.await_part(above, 1)
            self.send_part(above, 1, beside)
            self.to_pair(above, 1)

        def near(self):
            for part, half in ((beside, 1), (above, 0)):
                self.await_part(part, half)
                self.to_pair(part, half)

        def far(self):
            for half in range(2):
                self.await_part(across, half)
                self.to_pair(across, half)

        def await_pair(self):
            everything = self.at(pl.ds(0, section_count), self.other)
            await_bytes(everything, self.receive.at[section_count * 2])

        def drain(self):
            await_bytes(self.at(pl.ds(0, 3), self.place), self.send.at[0])
            await_bytes(self.at(pl.ds(0, section_count), self.place), self.send.at[1])

    def rows_gather(who):
        return Gather(
            lambda parts, place: rows_all.at[place, parts],
            who * 2 + core,
            who * 2 + 1 - core,
            capacity // 2,
            rows_send.at[who],
            rows_recv.at[who],
        )

    def guest_copies():
        copies = []
        for half in range(2):
            rows = rows_of(half, capacity // 2)
            copies.append(
                remote(
                    rows_all.at[core, section, rows, :],
                    rows_all.at[2 + core, section, rows, :],
                    guest_send.at[0],
                    rows_recv.at[1, section * 2 + half],
                    seq=host_spot * 2 + core,
                )
            )
        for half in range(2):
            copies.append(
                remote(
                    gate_rows.at[core],
                    gate_rows.at[2 + core],
                    gate_send.at[0],
                    gate_recv.at[1],
                    seq=host_spot * 2 + half,
                )
            )
        return copies

    def gate_copy(place):
        return remote(
            gate_rows.at[place], gate_rows.at[place], gate_send.at[0], gate_recv.at[0], seq=pair
        )

    def panel_copy(kind, place, send, target):
        piece = panel.at[kind, rows_of(place, chip_rows), :]
        return remote(piece, piece, send, panel_recv.at[kind, place], seq=target)

    def panel_to_pair(place):
        return panel_copy(core, place, panel_pair.at[place], pair)

    def panel_onward(who, host):
        return panel_copy(core, spots[who], panel_line.at[who, host - first], host * 2 + core)

    def later_hosts(body):
        def guarded(host):
            pl.when(host > spot)(lambda: body(host))

        repeat(first + 1, last + 1, guarded)

    def await_panel(kind, place):
        panel_copy(kind, place, panel_pair.at[place], pair).wait_recv()

    def earlier_spots(body):
        def guarded(step):
            place = last - 1 - step
            pl.when(host_of(place) < spot)(lambda: body(place))

        repeat(0, last, guarded)

    def heads_gather(head):
        return Gather(
            lambda parts, place: heads_all.at[place, head, parts],
            core,
            1 - core,
            chip_rows,
            heads_send.at[head],
            heads_recv.at[head],
        )

    def give_back(place, part, target):
        return remote(
            results.at[place, part],
            returned.at[core, part],
            back_send.at[0],
            back_recv.at[part],
            seq=target,
        )

    barrier = pltpu.get_barrier_semaphore()
    loads = [
        pltpu.make_async_copy(source, target, load_sems.at[number])
        for number, (source, target) in enumerate(
            (
                (tokens_hbm, mixed_ref),
                (chosen_hbm, chosen_ref),
                (gate_hbm, gate_ref),
                (gain_hbm, gain_ref),
                (count_hbm, count_ref),
            )
        )
    ]
    for load in loads:
        load.start()

    def greet(other):
        @pl.when((other != me) & (active | (other >= first * 2) & (other < (last + 1) * 2)))
        def _():
            pl.semaphore_signal(barrier, inc=1, device_id={"seq": other}, device_id_type=MESH)

    repeat(0, seq_count, greet)

    @pl.when(active)
    def _():
        for peer in (beside, above):
            pl.semaphore_signal(barrier, inc=1, device_id={"section": peer}, device_id_type=MESH)

    def pick(row_ref, index):
        row = row_ref[...]
        lane = lax.broadcasted_iota(jnp.int32, row.shape, 1)
        return jnp.sum(jnp.where(lane == index, row, 0), axis=1, keepdims=True)

    for load in loads:
        load.wait()
    for slot in range(slots):
        number = pick(chosen_ref, me * slots + slot)
        rows = mixed_ref[:BLOCK, :]
        gates = gate_ref[:1, :]
        for block in range(1, gate_ref.shape[0]):
            rows = jnp.where(
                jnp.broadcast_to(number, rows.shape) == block,
                mixed_ref[block * BLOCK : (block + 1) * BLOCK, :],
                rows,
            )
            gates = jnp.where(
                jnp.broadcast_to(number, gates.shape) == block,
                gate_ref[block : block + 1, :],
                gates,
            )
        rows_all[core, section, pl.ds(slot * BLOCK, BLOCK), :] = rows
        gate_rows[core, pl.ds(slot, 1), :] = gates

    pl.semaphore_wait(barrier, jnp.where(active, seq_count - 1 + 2, hosts * 2))

    @pl.when(jnp.logical_not(active))
    def _():
        for copy in guest_copies():
            copy.start()
        for chunk in chunks:
            send_weight(chunk)

    def gate_column(place):
        wide = gate_rows[place]
        square = lax.broadcasted_iota(jnp.int32, (BLOCK, BLOCK), 0) == lax.broadcasted_iota(
            jnp.int32, (BLOCK, BLOCK), 1
        )
        return jnp.concatenate(
            [
                jnp.sum(jnp.where(square, wide[slot : slot + 1, :], 0.0), axis=1, keepdims=True)
                for slot in range(slots)
            ],
            axis=0,
        )

    def normalise(place):
        square_sum = jnp.zeros((capacity, 1), jnp.float32)
        for part in range(section_count):
            features = rows_all[place, part].astype(jnp.float32)
            square_sum += jnp.sum(features * features, axis=-1, keepdims=True)
        factor = lax.rsqrt(square_sum / depth + EPSILON)
        for part in range(section_count):
            cols = pl.ds(part * width, width)
            normed_ref[rows_of(place, capacity), cols] = (
                rows_all[place, part].astype(jnp.float32) * factor * gain_ref[:, cols]
            ).astype(jnp.bfloat16)

    tile = tile_spots * chip_rows
    total = seq_count * capacity
    lane = lax.broadcasted_iota(jnp.int32, (1, tile), 1)

    def fill_slots(index):
        key_slot = lane + index * tile
        for piece in range(tile // BLOCK):
            place = index * (tile // BLOCK) + piece
            within = lax.rem(place, slots)
            count = jnp.broadcast_to(pick(count_ref, place // slots), (1, tile))
            key_slot = jnp.where((lane // BLOCK == piece) & (count <= within), total, key_slot)
        key_slots[pl.ds(index, 1), :] = key_slot

    scale = HEAD_DIM ** (-0.5)

    def offer(who):
        panel[core, rows_of(spots[who], chip_rows), :] = jnp.dot(
            normed_ref[rows_of(who, chip_rows), :],
            wkv[...].reshape(depth, kv_cols),
            preferred_element_type=jnp.float32,
        ).astype(jnp.bfloat16)
        panel_to_pair(spots[who]).start()
        later_hosts(lambda host: panel_onward(who, host).start())

    def ask(head):
        for who in range(2):
            queries_ref[head, rows_of(who, chip_rows), :] = jnp.dot(
                normed_ref[rows_of(who, chip_rows), :],
                wq[head].reshape(depth, HEAD_DIM),
                preferred_element_type=jnp.float32,
            ).astype(jnp.bfloat16)

    def fold(head, index):
        tall = lax.broadcasted_iota(jnp.int32, (host_rows, 1), 0)
        base = jnp.where(tall < chip_rows, spot * chip_rows, guest_spot * chip_rows - chip_rows)
        query_slot = tall + base
        key_slot = key_slots[pl.ds(index, 1), :]
        rows = rows_of(index, tile)
        if kv_cols == HEAD_DIM:
            cols = pl.ds(0, HEAD_DIM)
        else:
            cols = rows_of((core * heads_half + head) // ratio, HEAD_DIM)
        scores = (
            lax.dot_general(
                queries_ref[head],
                panel[0, rows, cols],
                (((1,), (1,)), ((), ())),
                preferred_element_type=jnp.float32,
            )
            * scale
        )
        weights = jnp.where(key_slot <= query_slot, jnp.exp(scores), 0.0)
        denom_ref[head] += jnp.sum(weights, axis=-1, keepdims=True)
        numer_ref[head] += jnp.dot(
            weights.astype(jnp.bfloat16), panel[1, rows, cols], preferred_element_type=jnp.float32
        )

    def fold_range(head, low, high):
        def body(index, carry):
            fold(head, index)
            return carry

        lax.fori_loop(low, high, body, 0)

    def settle(head):
        denom = denom_ref[head]
        safe = jnp.where(denom > 0, denom, 1.0)
        heads_all[core, head, section] = (numer_ref[head] / safe).astype(jnp.bfloat16)

    def finish(who, part):
        attended = [
            heads_all[half, head, source, rows_of(who, chip_rows), :]
            for source in range(section_count)
            for half in range(2)
            for head in range(heads_half)
        ]
        update = jnp.dot(
            jnp.concatenate(attended, axis=-1),
            wo[part].reshape(-1, part_o),
            preferred_element_type=jnp.float32,
        )
        cols = pl.ds(pl.multiple_of(core * half_o + part * part_o, part_o), part_o)
        for half in range(2):
            place = who * 2 + half
            fresh = (
                rows_all[place, section, :, cols].astype(jnp.float32)
                + gate_column(place) * update[half * capacity : (half + 1) * capacity]
            ).astype(out_ref.dtype)
            target = spots[who] * 2 + half
            if who == 0:
                pl.when(target == me)(lambda: out_ref.__setitem__((slice(None), cols), fresh))

            @pl.when(target != me)
            def _():
                results[place, part] = fresh
                give_back(place, part, target).start()

    early = 2

    @pl.when(active)
    def _():
        rows_gather(0).start()
        for chunk in chunks[:early]:
            send_weight(chunk)

        @pl.when(spot == last)
        def _():
            for chunk in chunks[early:]:
                send_weight(chunk)

        gate_copy(core).start()
        repeat(0, line // tile_spots, fill_slots)
        numer_ref[...] = jnp.zeros_like(numer_ref)
        denom_ref[...] = jnp.zeros_like(denom_ref)
        rows_gather(0).relay()
        pl.when(has_guest)(lambda: rows_gather(1).start(ready=True))
        rows_gather(0).near()
        rows_gather(0).far()
        pl.when(has_guest)(lambda: rows_gather(1).relay())
        normalise(core)
        rows_gather(0).await_pair()
        normalise(1 - core)
        receive_weight(chunks[0])
        offer(0)
        @pl.when(has_guest)
        def _():
            rows_gather(1).near()
            rows_gather(1).far()
            normalise(2 + core)
            rows_gather(1).await_pair()
            normalise(3 - core)
            offer(1)

        @pl.when(spot != last)
        def _():
            for chunk in chunks[early:]:
                send_weight(chunk)

        own_tile = spot // tile_spots
        farthest = jnp.where(has_guest, jnp.maximum(spot, guest_spot), spot)
        tiles = farthest // tile_spots + 1
        for head in range(heads_half):
            receive_weight((QUERY, head))
            ask(head)
            if head == 0:
                await_panel(1 - core, spot)
                pl.when(has_guest)(lambda: await_panel(1 - core, guest_spot))
            fold(head, own_tile)
            if head == 0:

                def pass_on(place):
                    await_panel(core, place)
                    panel_to_pair(place).start()

                earlier_spots(pass_on)
                earlier_spots(lambda place: await_panel(1 - core, place))
            fold_range(head, 0, own_tile)
            fold_range(head, own_tile + 1, tiles)
            settle(head)
            heads_gather(head).start()
            if head > 0:
                heads_gather(head - 1).relay()

        heads_gather(heads_half - 1).relay()
        gate_copy(1 - core).wait_recv()
        pl.when(has_guest)(lambda: await_bytes(gate_rows.at[pl.ds(2, 2)], gate_recv.at[1]))
        for head in range(heads_half):
            heads_gather(head).near()
        for head in range(heads_half):
            heads_gather(head).far()
        for head in range(heads_half):
            heads_gather(head).await_pair()
        for part in range(parts_o):
            receive_weight((OUT, part))
            pl.when(has_guest)(lambda: finish(1, part))
        for part in range(parts_o):
            finish(0, part)

        rows_gather(0).drain()
        for head in range(heads_half):
            heads_gather(head).drain()
        await_bytes(gate_rows.at[pl.ds(0, 1)], gate_send.at[0])
        panel_to_pair(spot).wait_send()
        later_hosts(lambda host: panel_onward(0, host).wait_send())
        earlier_spots(lambda place: panel_to_pair(place).wait_send())

        @pl.when(has_guest)
        def _():
            rows_gather(1).drain()
            panel_to_pair(guest_spot).wait_send()
            later_hosts(lambda host: panel_onward(1, host).wait_send())
            await_bytes(results.at[pl.ds(0, 3)], back_send.at[0])

        @pl.when(jnp.logical_not(has_guest))
        def _():
            await_bytes(results.at[pl.ds(0, 1)], back_send.at[0])

        for chunk in chunks:
            finish_weight(chunk, hosts * 2 - 1)
        for part in range(parts_o):
            cols = pl.ds(pl.multiple_of((1 - core) * half_o + part * part_o, part_o), part_o)
            await_bytes(returned.at[1 - core, part], back_recv.at[part])
            out_ref[:, cols] = returned[1 - core, part]

    @pl.when(jnp.logical_not(active))
    def _():
        await_bytes(rows_all.at[core, section], guest_send.at[0])
        await_bytes(gate_rows.at[pl.ds(0, 2)], gate_send.at[0])
        for chunk in chunks:
            finish_weight(chunk, hosts * 2)
        for part in range(parts_o):
            await_bytes(returned.at[pl.ds(0, 2), part], back_recv.at[part])
            for half in range(2):
                cols = pl.ds(half * half_o + part * part_o, part_o)
                out_ref[:, cols] = returned[half, part]

    for slot in range(slots):
        number = pick(chosen_ref, me * slots + slot)
        count = pick(count_ref, me)
        number = jnp.where(count > slot, number, gate_ref.shape[0])
        fresh = out_ref[slot * BLOCK : (slot + 1) * BLOCK, :]
        for block in range(gate_ref.shape[0]):
            rows = pl.ds(block * BLOCK, BLOCK)
            mixed_ref[rows, :] = jnp.where(
                jnp.broadcast_to(number, fresh.shape) == block, fresh, mixed_ref[rows, :]
            )


def local(
    tokens, norm_gain, w_query, w_key, w_value, w_out, router_gate, chosen_blocks, block_counts
):
    seq_count = lax.axis_size("seq")
    section_count = lax.axis_size("section")
    tok_rows, width = tokens.shape
    slots = chosen_blocks.shape[1]
    capacity = slots * BLOCK
    host_rows = 4 * capacity
    depth = section_count * width
    heads_half = w_query.shape[1] // 2 // HEAD_DIM
    parts_o = 2
    part_o = w_out.shape[1] // 2 // parts_o
    kv_cols = w_key.shape[1]
    line = seq_count // 2
    tile_spots = 2 if line == 4 else 1
    tile = tile_spots * 2 * capacity
    chunk_count = len(chunks_of(heads_half, parts_o))

    vmem = pl.BlockSpec(memory_space=pltpu.VMEM)
    anywhere = pl.BlockSpec(memory_space=pl.ANY)
    bf16 = jnp.bfloat16
    f32 = jnp.float32
    dma = pltpu.SemaphoreType.DMA
    blocks = chosen_blocks.reshape(-1)
    return pl.pallas_call(
        functools.partial(kernel, seq_count, section_count, tile_spots),
        out_shape=pltpu.VMEM(tokens.shape, tokens.dtype),
        in_specs=[anywhere] * 9,
        out_specs=vmem,
        scratch_shapes=[
            pltpu.VMEM((1, depth), f32),
            pltpu.VMEM((tok_rows // BLOCK, BLOCK), f32),
            pltpu.VMEM((1, blocks.shape[0]), jnp.int32),
            pltpu.VMEM((1, seq_count), jnp.int32),
            pltpu.VMEM((capacity, width), bf16),
            pltpu.VMEM((4, section_count, capacity, width), bf16),
            pltpu.VMEM((4, slots, BLOCK), f32),
            pltpu.VMEM((host_rows, depth), bf16),
            pltpu.VMEM((seq_count, w_key.shape[0], kv_cols), bf16),
            pltpu.VMEM((heads_half, seq_count, w_query.shape[0], HEAD_DIM), bf16),
            pltpu.VMEM((parts_o, seq_count, w_out.shape[0], part_o), bf16),
            pltpu.VMEM((2, seq_count * capacity, kv_cols), bf16),
            pltpu.VMEM((heads_half, host_rows, HEAD_DIM), bf16),
            pltpu.VMEM((heads_half, host_rows, HEAD_DIM), f32),
            pltpu.VMEM((heads_half, host_rows, 1), f32),
            pltpu.VMEM((2, heads_half, section_count, host_rows, HEAD_DIM), bf16),
            pltpu.VMEM((4, parts_o, capacity, part_o), bf16),
            pltpu.VMEM((2, parts_o, capacity, part_o), bf16),
            pltpu.VMEM((line // tile_spots, tile), jnp.int32),
            dma((5,)),
            dma((chunk_count,)),
            dma((chunk_count,)),
            dma((1,)),
            dma((2, 2)),
            dma((2, section_count * 2 + 1)),
            dma((1,)),
            dma((2,)),
            dma((2, line - 2)),
            dma((line,)),
            dma((2, line)),
            dma((heads_half, 2)),
            dma((heads_half, section_count * 2 + 1)),
            dma((1,)),
            dma((parts_o,)),
        ],
        compiler_params=pltpu.CompilerParams(collective_id=0, has_side_effects=True),
    )(
        tokens,
        norm_gain[None, :],
        router_gate.reshape(tok_rows // BLOCK, BLOCK),
        blocks[None, :],
        block_counts[None, :],
        w_query,
        w_key,
        w_value,
        w_out,
    )


def solution(mesh):
    return jax.shard_map(
        local,
        mesh=mesh,
        in_specs=(
            P("seq", "section"),
            P(),
            P("seq", "section"),
            P("seq", "section"),
            P("seq", "section"),
            P("seq", "section"),
            P("seq"),
            P(),
            P(),
        ),
        out_specs=P("seq", "section"),
        check_vma=False,
    )
```

```python
import functools

import jax
import jax.numpy as jnp
from jax import lax
from jax.experimental import pallas as pl
from jax.experimental.pallas import tpu as pltpu
from jax.sharding import PartitionSpec as P

HEADS = 16
KV_HEADS = 4
HEAD_DIM = 128
BLOCK = 128
EPSILON = 1e-05
MESH = pl.DeviceIdType.MESH

KV, QUERY, OUT = range(3)


def chunks_of(heads_half, parts_o):
    chunks = [(KV, 0)]
    chunks += [(QUERY, head) for head in range(heads_half)]
    chunks += [(OUT, part) for part in range(parts_o)]
    return chunks


def repeat(low, high, body):
    if high - low <= 8:
        for step in range(low, high):
            body(step)
    else:

        def wrapped(step, carry):
            body(step)
            return carry

        lax.fori_loop(low, high, wrapped, 0)


def kernel(
    seq_count,
    section_count,
    tile_spots,
    tokens_hbm,
    gain_hbm,
    gate_hbm,
    chosen_hbm,
    count_hbm,
    wq_in,
    wk_in,
    wv_in,
    wo_in,
    mixed_ref,
    gain_ref,
    gate_ref,
    chosen_ref,
    count_ref,
    out_ref,
    rows_all,
    gate_rows,
    normed_ref,
    wkv,
    wq,
    wo,
    panel,
    queries_ref,
    numer_ref,
    denom_ref,
    heads_all,
    results,
    returned,
    key_slots,
    load_sems,
    weight_send,
    weight_recv,
    guest_send,
    rows_send,
    rows_recv,
    gate_send,
    gate_recv,
    panel_line,
    panel_pair,
    panel_recv,
    heads_send,
    heads_recv,
    back_send,
    back_recv,
):
    me = lax.axis_index("seq")
    section = lax.axis_index("section")
    line = seq_count // 2
    spot = me // 2
    core = lax.rem(me, 2)
    pair = spot * 2 + 1 - core
    slots = chosen_ref.shape[1] // seq_count
    capacity, width = out_ref.shape
    chip_rows = 2 * capacity
    host_rows = 2 * chip_rows
    kv_cols = wk_in.shape[1]
    ratio = HEADS // KV_HEADS
    half_q = wq_in.shape[1] // 2
    heads_half = half_q // HEAD_DIM
    half_o = wo_in.shape[1] // 2
    parts_o, _, _, part_o = wo.shape
    depth = section_count * width
    chunks = chunks_of(heads_half, parts_o)
    number_of = {chunk: number for number, chunk in enumerate(chunks)}
    first, last = 1, line - 2
    hosts = last - first + 1
    active = (spot >= first) & (spot <= last)
    has_guest = (spot == first) | (spot == last)
    near = jnp.where(spot * 2 < line, 1, -1)
    guest_spot = spot - near
    host_spot = spot + near
    spots = (spot, guest_spot)
    beside = section + 1 - 2 * lax.rem(section, 2)
    above = lax.rem(section + 2, section_count)
    across = section_count - 1 - section

    def host_of(place):
        if isinstance(place, int):
            return min(max(place, first), last)
        return jnp.clip(place, first, last)

    def rows_of(block, size):
        if isinstance(block, int):
            return pl.ds(block * size, size)
        return pl.ds(pl.multiple_of(block * size, size), size)

    def remote(src, dst, send, receive, **device):
        return pltpu.make_async_remote_copy(
            src_ref=src,
            dst_ref=dst,
            send_sem=send,
            recv_sem=receive,
            device_id=device,
            device_id_type=MESH,
        )

    def await_bytes(ref, sem):
        pltpu.make_async_copy(ref, ref, sem).wait()

    def weight_from(chunk, half):
        kind, part = chunk
        if kind == KV:
            return (wk_in, wv_in)[half]
        if kind == QUERY:
            return wq_in.at[:, pl.ds(half * half_q + part * HEAD_DIM, HEAD_DIM)]
        return wo_in.at[:, pl.ds(half * half_o + part * part_o, part_o)]

    def weight_to(chunk, low, count):
        kind, part = chunk
        blocks = pl.ds(low, count)
        if kind == KV:
            return wkv.at[blocks]
        if kind == QUERY:
            return wq.at[part, blocks]
        return wo.at[part, blocks]

    def weight_copy(chunk, half, target):
        number = number_of[chunk]
        return remote(
            weight_from(chunk, half),
            weight_to(chunk, me, 1).at[0],
            weight_send.at[number],
            weight_recv.at[number],
            seq=target,
        )

    def send_weight(chunk):
        def body(host):
            for half in range(2):
                target = host * 2 + half

                @pl.when(target != me)
                def _():
                    weight_copy(chunk, half, target).start()

                @pl.when(target == me)
                def _():
                    pltpu.make_async_copy(
                        weight_from(chunk, half),
                        weight_to(chunk, me, 1).at[0],
                        weight_recv.at[number_of[chunk]],
                    ).start()

        repeat(first, last + 1, body)

    def receive_weight(chunk):
        await_bytes(weight_to(chunk, 0, seq_count), weight_recv.at[number_of[chunk]])

    def finish_weight(chunk, count):
        await_bytes(weight_to(chunk, 0, count), weight_send.at[number_of[chunk]])

    class Gather:
        def __init__(self, at, place, other, rows, send, receive):
            self.at, self.place, self.other, self.rows = at, place, other, rows
            self.send, self.receive = send, receive

        def copy(self, part, half, send, receive, **device):
            piece = self.at(pl.ds(part, 1), self.place).at[0].at[rows_of(half, self.rows)]
            return remote(piece, piece, send, receive, **device)

        def send_part(self, part, half, peer):
            receive = self.receive.at[part * 2 + half]
            self.copy(part, half, self.send.at[0], receive, section=peer).start()

        def await_part(self, part, half):
            receive = self.receive.at[part * 2 + half]
            self.copy(part, half, self.send.at[0], receive, seq=pair).wait_recv()

        def to_pair(self, part, half):
            receive = self.receive.at[section_count * 2]
            self.copy(part, half, self.send.at[1], receive, seq=pair).start()

        def start(self, ready=False):
            if ready:
                self.await_part(section, 0)
            self.send_part(section, 0, beside)
            if ready:
                self.await_part(section, 1)
            self.send_part(section, 1, above)
            self.send_part(section, 1, beside)
            self.send_part(section, 0, above)
            self.to_pair(section, 0)
            self.to_pair(section, 1)

        def relay(self):
            self.await_part(beside, 0)
            self.send_part(beside, 0, above)
            self.to_pair(beside, 0)
            self.await_part(above, 1)
            self.send_part(above, 1, beside)
            self.to_pair(above, 1)

        def near(self):
            for part, half in ((beside, 1), (above, 0)):
                self.await_part(part, half)
                self.to_pair(part, half)

        def far(self):
            for half in range(2):
                self.await_part(across, half)
                self.to_pair(across, half)

        def await_pair(self):
            everything = self.at(pl.ds(0, section_count), self.other)
            await_bytes(everything, self.receive.at[section_count * 2])

        def drain(self):
            await_bytes(self.at(pl.ds(0, 3), self.place), self.send.at[0])
            await_bytes(self.at(pl.ds(0, section_count), self.place), self.send.at[1])

    def rows_gather(who):
        return Gather(
            lambda parts, place: rows_all.at[place, parts],
            who * 2 + core,
            who * 2 + 1 - core,
            capacity // 2,
            rows_send.at[who],
            rows_recv.at[who],
        )

    def guest_copies():
        copies = []
        for half in range(2):
            rows = rows_of(half, capacity // 2)
            copies.append(
                remote(
                    rows_all.at[core, section, rows, :],
                    rows_all.at[2 + core, section, rows, :],
                    guest_send.at[0],
                    rows_recv.at[1, section * 2 + half],
                    seq=host_spot * 2 + core,
                )
            )
        for half in range(2):
            copies.append(
                remote(
                    gate_rows.at[core],
                    gate_rows.at[2 + core],
                    gate_send.at[0],
                    gate_recv.at[1],
                    seq=host_spot * 2 + half,
                )
            )
        return copies

    def gate_copy(place):
        return remote(
            gate_rows.at[place], gate_rows.at[place], gate_send.at[0], gate_recv.at[0], seq=pair
        )

    def panel_copy(kind, place, send, target):
        piece = panel.at[kind, rows_of(place, chip_rows), :]
        return remote(piece, piece, send, panel_recv.at[kind, place], seq=target)

    def panel_to_pair(place):
        return panel_copy(core, place, panel_pair.at[place], pair)

    def panel_onward(who, host):
        return panel_copy(core, spots[who], panel_line.at[who, host - first], host * 2 + core)

    def later_hosts(body):
        def guarded(host):
            pl.when(host > spot)(lambda: body(host))

        repeat(first + 1, last + 1, guarded)

    def await_panel(kind, place):
        panel_copy(kind, place, panel_pair.at[place], pair).wait_recv()

    def earlier_spots(body):
        def guarded(step):
            place = last - 1 - step
            pl.when(host_of(place) < spot)(lambda: body(place))

        repeat(0, last, guarded)

    def heads_gather(head):
        return Gather(
            lambda parts, place: heads_all.at[place, head, parts],
            core,
            1 - core,
            chip_rows,
            heads_send.at[head],
            heads_recv.at[head],
        )

    def give_back(place, part, target):
        return remote(
            results.at[place, part],
            returned.at[core, part],
            back_send.at[0],
            back_recv.at[part],
            seq=target,
        )

    barrier = pltpu.get_barrier_semaphore()
    loads = [
        pltpu.make_async_copy(source, target, load_sems.at[number])
        for number, (source, target) in enumerate(
            (
                (tokens_hbm, mixed_ref),
                (chosen_hbm, chosen_ref),
                (gate_hbm, gate_ref),
                (gain_hbm, gain_ref),
                (count_hbm, count_ref),
            )
        )
    ]
    for load in loads:
        load.start()

    def greet(other):
        @pl.when((other != me) & (active | (other >= first * 2) & (other < (last + 1) * 2)))
        def _():
            pl.semaphore_signal(barrier, inc=1, device_id={"seq": other}, device_id_type=MESH)

    repeat(0, seq_count, greet)

    @pl.when(active)
    def _():
        for peer in (beside, above):
            pl.semaphore_signal(barrier, inc=1, device_id={"section": peer}, device_id_type=MESH)

    def pick(row_ref, index):
        row = row_ref[...]
        lane = lax.broadcasted_iota(jnp.int32, row.shape, 1)
        return jnp.sum(jnp.where(lane == index, row, 0), axis=1, keepdims=True)

    for load in loads:
        load.wait()
    for slot in range(slots):
        number = pick(chosen_ref, me * slots + slot)
        rows = mixed_ref[:BLOCK, :]
        gates = gate_ref[:1, :]
        for block in range(1, gate_ref.shape[0]):
            rows = jnp.where(
                jnp.broadcast_to(number, rows.shape) == block,
                mixed_ref[block * BLOCK : (block + 1) * BLOCK, :],
                rows,
            )
            gates = jnp.where(
                jnp.broadcast_to(number, gates.shape) == block,
                gate_ref[block : block + 1, :],
                gates,
            )
        rows_all[core, section, pl.ds(slot * BLOCK, BLOCK), :] = rows
        gate_rows[core, pl.ds(slot, 1), :] = gates

    pl.semaphore_wait(barrier, jnp.where(active, seq_count - 1 + 2, hosts * 2))

    @pl.when(jnp.logical_not(active))
    def _():
        for copy in guest_copies():
            copy.start()
        for chunk in chunks:
            send_weight(chunk)

    def settle_cols(cols):
        for slot in range(slots):
            number = pick(chosen_ref, me * slots + slot)
            number = jnp.where(pick(count_ref, me) > slot, number, gate_ref.shape[0])
            fresh = out_ref[slot * BLOCK : (slot + 1) * BLOCK, cols]
            for block in range(gate_ref.shape[0]):
                rows = pl.ds(block * BLOCK, BLOCK)
                mixed_ref[rows, cols] = jnp.where(
                    jnp.broadcast_to(number, fresh.shape) == block, fresh, mixed_ref[rows, cols]
                )

    def gate_column(place):
        wide = gate_rows[place]
        square = lax.broadcasted_iota(jnp.int32, (BLOCK, BLOCK), 0) == lax.broadcasted_iota(
            jnp.int32, (BLOCK, BLOCK), 1
        )
        return jnp.concatenate(
            [
                jnp.sum(jnp.where(square, wide[slot : slot + 1, :], 0.0), axis=1, keepdims=True)
                for slot in range(slots)
            ],
            axis=0,
        )

    def normalise(place):
        square_sum = jnp.zeros((capacity, 1), jnp.float32)
        for part in range(section_count):
            features = rows_all[place, part].astype(jnp.float32)
            square_sum += jnp.sum(features * features, axis=-1, keepdims=True)
        factor = lax.rsqrt(square_sum / depth + EPSILON)
        for part in range(section_count):
            cols = pl.ds(part * width, width)
            normed_ref[rows_of(place, capacity), cols] = (
                rows_all[place, part].astype(jnp.float32) * factor * gain_ref[:, cols]
            ).astype(jnp.bfloat16)

    tile = tile_spots * chip_rows
    total = seq_count * capacity
    lane = lax.broadcasted_iota(jnp.int32, (1, tile), 1)

    def fill_slots(index):
        key_slot = lane + index * tile
        for piece in range(tile // BLOCK):
            place = index * (tile // BLOCK) + piece
            within = lax.rem(place, slots)
            count = jnp.broadcast_to(pick(count_ref, place // slots), (1, tile))
            key_slot = jnp.where((lane // BLOCK == piece) & (count <= within), total, key_slot)
        key_slots[pl.ds(index, 1), :] = key_slot

    scale = HEAD_DIM ** (-0.5)

    def offer(who):
        panel[core, rows_of(spots[who], chip_rows), :] = jnp.dot(
            normed_ref[rows_of(who, chip_rows), :],
            wkv[...].reshape(depth, kv_cols),
            preferred_element_type=jnp.float32,
        ).astype(jnp.bfloat16)
        panel_to_pair(spots[who]).start()
        later_hosts(lambda host: panel_onward(who, host).start())

    def ask(head):
        for who in range(2):
            queries_ref[head, rows_of(who, chip_rows), :] = jnp.dot(
                normed_ref[rows_of(who, chip_rows), :],
                wq[head].reshape(depth, HEAD_DIM),
                preferred_element_type=jnp.float32,
            ).astype(jnp.bfloat16)

    def fold(head, index):
        tall = lax.broadcasted_iota(jnp.int32, (host_rows, 1), 0)
        base = jnp.where(tall < chip_rows, spot * chip_rows, guest_spot * chip_rows - chip_rows)
        query_slot = tall + base
        key_slot = key_slots[pl.ds(index, 1), :]
        rows = rows_of(index, tile)
        if kv_cols == HEAD_DIM:
            cols = pl.ds(0, HEAD_DIM)
        else:
            cols = rows_of((core * heads_half + head) // ratio, HEAD_DIM)
        scores = (
            lax.dot_general(
                queries_ref[head],
                panel[0, rows, cols],
                (((1,), (1,)), ((), ())),
                preferred_element_type=jnp.float32,
            )
            * scale
        )
        weights = jnp.where(key_slot <= query_slot, jnp.exp(scores), 0.0)
        denom_ref[head] += jnp.sum(weights, axis=-1, keepdims=True)
        numer_ref[head] += jnp.dot(
            weights.astype(jnp.bfloat16), panel[1, rows, cols], preferred_element_type=jnp.float32
        )

    def fold_range(head, low, high):
        def body(index, carry):
            fold(head, index)
            return carry

        lax.fori_loop(low, high, body, 0)

    def settle(head):
        denom = denom_ref[head]
        safe = jnp.where(denom > 0, denom, 1.0)
        heads_all[core, head, section] = (numer_ref[head] / safe).astype(jnp.bfloat16)

    def finish(who, part):
        attended = [
            heads_all[half, head, source, rows_of(who, chip_rows), :]
            for source in range(section_count)
            for half in range(2)
            for head in range(heads_half)
        ]
        update = jnp.dot(
            jnp.concatenate(attended, axis=-1),
            wo[part].reshape(-1, part_o),
            preferred_element_type=jnp.float32,
        )
        cols = pl.ds(pl.multiple_of(core * half_o + part * part_o, part_o), part_o)
        for half in range(2):
            place = who * 2 + half
            fresh = (
                rows_all[place, section, :, cols].astype(jnp.float32)
                + gate_column(place) * update[half * capacity : (half + 1) * capacity]
            ).astype(out_ref.dtype)
            target = spots[who] * 2 + half
            if who == 0:
                pl.when(target == me)(lambda: out_ref.__setitem__((slice(None), cols), fresh))

            @pl.when(target != me)
            def _():
                results[place, part] = fresh
                give_back(place, part, target).start()

    early = 2

    @pl.when(active)
    def _():
        rows_gather(0).start()
        for chunk in chunks[:early]:
            send_weight(chunk)

        @pl.when(spot == last)
        def _():
            for chunk in chunks[early:]:
                send_weight(chunk)

        gate_copy(core).start()
        repeat(0, line // tile_spots, fill_slots)
        numer_ref[...] = jnp.zeros_like(numer_ref)
        denom_ref[...] = jnp.zeros_like(denom_ref)
        rows_gather(0).relay()
        pl.when(has_guest)(lambda: rows_gather(1).start(ready=True))
        rows_gather(0).near()
        rows_gather(0).far()
        pl.when(has_guest)(lambda: rows_gather(1).relay())
        normalise(core)
        rows_gather(0).await_pair()
        normalise(1 - core)
        receive_weight(chunks[0])
        offer(0)
        @pl.when(has_guest)
        def _():
            rows_gather(1).near()
            rows_gather(1).far()
            normalise(2 + core)
            rows_gather(1).await_pair()
            normalise(3 - core)
            offer(1)

        @pl.when(spot != last)
        def _():
            for chunk in chunks[early:]:
                send_weight(chunk)

        own_tile = spot // tile_spots
        farthest = jnp.where(has_guest, jnp.maximum(spot, guest_spot), spot)
        tiles = farthest // tile_spots + 1
        for head in range(heads_half):
            receive_weight((QUERY, head))
            ask(head)
            if head == 0:
                await_panel(1 - core, spot)
                pl.when(has_guest)(lambda: await_panel(1 - core, guest_spot))
            fold(head, own_tile)
            if head == 0:

                def pass_on(place):
                    await_panel(core, place)
                    panel_to_pair(place).start()

                earlier_spots(pass_on)
                earlier_spots(lambda place: await_panel(1 - core, place))
            fold_range(head, 0, own_tile)
            fold_range(head, own_tile + 1, tiles)
            settle(head)
            heads_gather(head).start()
            if head > 0:
                heads_gather(head - 1).relay()

        heads_gather(heads_half - 1).relay()
        gate_copy(1 - core).wait_recv()
        pl.when(has_guest)(lambda: await_bytes(gate_rows.at[pl.ds(2, 2)], gate_recv.at[1]))
        for head in range(heads_half):
            heads_gather(head).near()
        for head in range(heads_half):
            heads_gather(head).far()
        for head in range(heads_half):
            heads_gather(head).await_pair()
        for part in range(parts_o):
            receive_weight((OUT, part))
            pl.when(has_guest)(lambda: finish(1, part))
        for part in range(parts_o):
            finish(0, part)

        rows_gather(0).drain()
        for head in range(heads_half):
            heads_gather(head).drain()
        await_bytes(gate_rows.at[pl.ds(0, 1)], gate_send.at[0])
        panel_to_pair(spot).wait_send()
        later_hosts(lambda host: panel_onward(0, host).wait_send())
        earlier_spots(lambda place: panel_to_pair(place).wait_send())

        @pl.when(has_guest)
        def _():
            rows_gather(1).drain()
            panel_to_pair(guest_spot).wait_send()
            later_hosts(lambda host: panel_onward(1, host).wait_send())
            await_bytes(results.at[pl.ds(0, 3)], back_send.at[0])

        @pl.when(jnp.logical_not(has_guest))
        def _():
            await_bytes(results.at[pl.ds(0, 1)], back_send.at[0])

        for chunk in chunks:
            finish_weight(chunk, hosts * 2 - 1)
        for part in range(parts_o):
            cols = pl.ds(pl.multiple_of((1 - core) * half_o + part * part_o, part_o), part_o)
            own = pl.ds(pl.multiple_of(core * half_o + part * part_o, part_o), part_o)
            settle_cols(own)
            await_bytes(returned.at[1 - core, part], back_recv.at[part])
            out_ref[:, cols] = returned[1 - core, part]
            settle_cols(cols)

    @pl.when(jnp.logical_not(active))
    def _():
        await_bytes(rows_all.at[core, section], guest_send.at[0])
        await_bytes(gate_rows.at[pl.ds(0, 2)], gate_send.at[0])
        for chunk in chunks:
            finish_weight(chunk, hosts * 2)
        for part in range(parts_o):
            await_bytes(returned.at[pl.ds(0, 2), part], back_recv.at[part])
            for half in range(2):
                cols = pl.ds(half * half_o + part * part_o, part_o)
                out_ref[:, cols] = returned[half, part]
                settle_cols(cols)


def local(
    tokens, norm_gain, w_query, w_key, w_value, w_out, router_gate, chosen_blocks, block_counts
):
    seq_count = lax.axis_size("seq")
    section_count = lax.axis_size("section")
    tok_rows, width = tokens.shape
    slots = chosen_blocks.shape[1]
    capacity = slots * BLOCK
    host_rows = 4 * capacity
    depth = section_count * width
    heads_half = w_query.shape[1] // 2 // HEAD_DIM
    parts_o = 2
    part_o = w_out.shape[1] // 2 // parts_o
    kv_cols = w_key.shape[1]
    line = seq_count // 2
    tile_spots = 2 if line == 4 else 1
    tile = tile_spots * 2 * capacity
    chunk_count = len(chunks_of(heads_half, parts_o))

    vmem = pl.BlockSpec(memory_space=pltpu.VMEM)
    anywhere = pl.BlockSpec(memory_space=pl.ANY)
    bf16 = jnp.bfloat16
    f32 = jnp.float32
    dma = pltpu.SemaphoreType.DMA
    blocks = chosen_blocks.reshape(-1)
    return pl.pallas_call(
        functools.partial(kernel, seq_count, section_count, tile_spots),
        out_shape=pltpu.VMEM(tokens.shape, tokens.dtype),
        in_specs=[anywhere] * 9,
        out_specs=vmem,
        scratch_shapes=[
            pltpu.VMEM((1, depth), f32),
            pltpu.VMEM((tok_rows // BLOCK, BLOCK), f32),
            pltpu.VMEM((1, blocks.shape[0]), jnp.int32),
            pltpu.VMEM((1, seq_count), jnp.int32),
            pltpu.VMEM((capacity, width), bf16),
            pltpu.VMEM((4, section_count, capacity, width), bf16),
            pltpu.VMEM((4, slots, BLOCK), f32),
            pltpu.VMEM((host_rows, depth), bf16),
            pltpu.VMEM((seq_count, w_key.shape[0], kv_cols), bf16),
            pltpu.VMEM((heads_half, seq_count, w_query.shape[0], HEAD_DIM), bf16),
            pltpu.VMEM((parts_o, seq_count, w_out.shape[0], part_o), bf16),
            pltpu.VMEM((2, seq_count * capacity, kv_cols), bf16),
            pltpu.VMEM((heads_half, host_rows, HEAD_DIM), bf16),
            pltpu.VMEM((heads_half, host_rows, HEAD_DIM), f32),
            pltpu.VMEM((heads_half, host_rows, 1), f32),
            pltpu.VMEM((2, heads_half, section_count, host_rows, HEAD_DIM), bf16),
            pltpu.VMEM((4, parts_o, capacity, part_o), bf16),
            pltpu.VMEM((2, parts_o, capacity, part_o), bf16),
            pltpu.VMEM((line // tile_spots, tile), jnp.int32),
            dma((5,)),
            dma((chunk_count,)),
            dma((chunk_count,)),
            dma((1,)),
            dma((2, 2)),
            dma((2, section_count * 2 + 1)),
            dma((1,)),
            dma((2,)),
            dma((2, line - 2)),
            dma((line,)),
            dma((2, line)),
            dma((heads_half, 2)),
            dma((heads_half, section_count * 2 + 1)),
            dma((1,)),
            dma((parts_o,)),
        ],
        compiler_params=pltpu.CompilerParams(collective_id=0, has_side_effects=True),
    )(
        tokens,
        norm_gain[None, :],
        router_gate.reshape(tok_rows // BLOCK, BLOCK),
        blocks[None, :],
        block_counts[None, :],
        w_query,
        w_key,
        w_value,
        w_out,
    )


def solution(mesh):
    return jax.shard_map(
        local,
        mesh=mesh,
        in_specs=(
            P("seq", "section"),
            P(),
            P("seq", "section"),
            P("seq", "section"),
            P("seq", "section"),
            P("seq", "section"),
            P("seq"),
            P(),
            P(),
        ),
        out_specs=P("seq", "section"),
        check_vma=False,
    )
```
